32 devices in a mesh: row: 4 (over y, x), col: 8 (over z, core).
Axes of the slice: x: 2, y: 2, z: 4, core: 2. Of those that a mesh axis runs over, the one named last changes fastest.
Arguments:
- objects: float32 [4, 2048, 4096], P(None, 'row', 'col'), may hold values from -5 to 5
- illumination: float32 [2, 256, 256], replicated, may hold values from -5 to 5
- propagator_phase: float32 [256, 256], replicated, may hold values from -3.140625 to 3.140625
- intensity: bfloat16 [384, 256, 256], P(('row', 'col')), may hold values from 0 to 2
- offsets: int32 [384, 2], P(('row', 'col')), may hold values from -1 to 3, as said below
- counts: int32 [32], P(('row', 'col')), may hold values from 0 to 12, as said below
Outputs:
- gradient: float32 [4, 2048, 4096], P(None, 'row', 'col')
The draws below stay inside these ranges and needn't reach their ends.
Inputs may be any that keep to these rules, and one draw needn't show every extreme that they name: `counts`: for every device, its count plus the count of the device 8 // 2 further along col (cyclically, same row) is at most 12; some device has exactly 12; every device at row index 0 has a live slot. `offsets`: the first slot of every device has column offset 512 // 128 - 1.
All inputs are finite; a program needn't handle non-finite values.
Results may differ from the reference program's by a relative error of at most 0.015.
Values may be sent and summed in bfloat16 or wider, within the bound.
No kernel may reach another device: no remote copies, remote signals or barrier semaphores. Data moves between devices by JAX's collectives and lax.ppermute only.
A program may use at most 128 MiB of HBM per device.

```python
import math
import jax
import jax.numpy as jnp
from jax import lax

PROBE = 256
TILE = 512
SLOTS = 12
NR = 2048
NC = 4096
TASKS = 384
N_ROW = 4
N_COL = 8


def draw_counts(key, part):
    half_cols = N_COL // 2
    pair_count = N_ROW * half_cols
    key_total, key_share, key_pick, key_side = jax.random.split(jax.random.fold_in(key, 11), 4)
    totals = jax.random.randint(key_total, (pair_count,), 3 * SLOTS // 4, SLOTS + 1)
    shares = jax.random.randint(key_share, (pair_count,), 1, totals)
    chosen = jax.random.randint(key_pick, (), half_cols, pair_count)
    flip_side = jax.random.randint(key_side, (), 0, 2)
    pair_ids = jnp.arange(pair_count)
    totals = jnp.where(pair_ids == chosen, SLOTS, totals)
    shares = jnp.where(pair_ids == chosen, SLOTS * flip_side, shares)
    first_half = shares.reshape(N_ROW, half_cols)
    second_half = (totals - shares).reshape(N_ROW, half_cols)
    return jnp.concatenate([first_half, second_half], axis=1).reshape(N_ROW * N_COL).astype(jnp.int32)


def draw_offsets(key, part):
    highest = TILE // (PROBE // 2)
    drawn = jax.random.randint(jax.random.fold_in(key, 23), (TASKS, 2), -1, highest)
    first_slot = jnp.arange(TASKS) % SLOTS == 0
    column = jnp.where(first_slot, highest - 1, drawn[:, 1])
    return jnp.stack([drawn[:, 0], column], axis=1).astype(jnp.int32)


def block_scale(stream_key, shape, cuts, low, high):
    loudness, own = 1.0, jax.random.fold_in(stream_key, 6)
    for position, blocks in cuts:
        draws = jnp.exp(jax.random.uniform(jax.random.fold_in(own, position), (blocks,), jnp.float32, low / len(cuts), high / len(cuts)))
        loudness = loudness * jnp.repeat(draws, shape[position] // blocks).reshape([-1 if axis == position else 1 for axis in range(len(shape))])
    return loudness


def centred(key, dims, width, reach, cuts=(), kind=jnp.bfloat16):
    entries = jax.random.normal(key, dims, jnp.float32) * width
    if len(cuts) > 0:
        entries = block_scale(key, dims, cuts, -0.22, 0.18) * entries
    return jnp.clip(entries, min=-reach, max=reach).astype(kind)


def setup_inputs(seed: int = 0) -> dict:
    arg_keys = jax.random.split(jax.random.key(seed), 7)
    objects = centred(arg_keys[0], (4, NR, NC), 0.7, 5.0, ((1, 4), (2, 8)), jnp.float32)
    illumination = centred(arg_keys[1], (2, PROBE, PROBE), 0.7, 5.0, (), jnp.float32)
    propagator_phase = jnp.clip(jax.random.uniform(arg_keys[2], (PROBE, PROBE), jnp.float32, -3.140625, 3.140625), -3.140625, 3.140625)
    intensity = jnp.clip(2.0 * jax.random.uniform(arg_keys[3], (TASKS, PROBE, PROBE), jnp.float32) ** block_scale(arg_keys[3], (TASKS, PROBE, PROBE), ((0, 32),), -0.2, 0.2), 0.0, 2.0).astype(jnp.bfloat16)
    offsets = draw_offsets(jax.random.fold_in(arg_keys[6], 71), 0)
    counts = draw_counts(jax.random.fold_in(arg_keys[6], 71), 0)
    return dict(objects=objects, illumination=illumination, propagator_phase=propagator_phase, intensity=intensity, offsets=offsets, counts=counts)


def tables(extent):
    number = jnp.arange(extent, dtype=jnp.int32)
    turns = number[:, None] * number[None, :] % extent
    angle = turns.astype(jnp.float32) * (2.0 * math.pi / extent)
    scale = 1.0 / math.sqrt(extent)
    return ((jnp.cos(angle) * scale).astype(jnp.bfloat16), (jnp.sin(angle) * scale).astype(jnp.bfloat16))

def left_product(matrix, field):
    return jnp.einsum('jk,bkl->bjl', matrix.astype(jnp.float32), field.astype(jnp.float32))

def right_product(field, matrix):
    return jnp.einsum('bjk,kl->bjl', field.astype(jnp.float32), matrix.astype(jnp.float32))

def transform(field_real, field_imag, direction, cosine_table, sine_table):
    upper_real = (left_product(cosine_table, field_real) + direction * left_product(sine_table, field_imag)).astype(jnp.bfloat16)
    upper_imag = (left_product(cosine_table, field_imag) - direction * left_product(sine_table, field_real)).astype(jnp.bfloat16)
    out_real = right_product(upper_real, cosine_table) + direction * right_product(upper_imag, sine_table)
    out_imag = right_product(upper_imag, cosine_table) - direction * right_product(upper_real, sine_table)
    return (out_real, out_imag)

def complex_product(left_real, left_imag, right_real, right_imag):
    return (left_real * right_real - left_imag * right_imag, left_real * right_imag + left_imag * right_real)

def to_half(pair):
    return (pair[0].astype(jnp.bfloat16), pair[1].astype(jnp.bfloat16))

def slot_gradient(illumination, propagator_phase, patches, intensity, cosine_table, sine_table):
    light_real = illumination[0]
    light_imag = illumination[1]
    spread_real = jnp.cos(propagator_phase)
    spread_imag = jnp.sin(propagator_phase)
    first_real = patches[:, 0].astype(jnp.float32)
    first_imag = patches[:, 1].astype(jnp.float32)
    second_real = patches[:, 2].astype(jnp.float32)
    second_imag = patches[:, 3].astype(jnp.float32)
    wave_real, wave_imag = to_half(complex_product(light_real, light_imag, first_real, first_imag))
    front_real, front_imag = transform(wave_real, wave_imag, 1.0, cosine_table, sine_table)
    mixed_real, mixed_imag = to_half(complex_product(spread_real, spread_imag, front_real, front_imag))
    passed_real, passed_imag = transform(mixed_real, mixed_imag, -1.0, cosine_table, sine_table)
    wave2_real, wave2_imag = to_half(complex_product(passed_real, passed_imag, second_real, second_imag))
    far_real, far_imag = transform(wave2_real, wave2_imag, 1.0, cosine_table, sine_table)
    misfit = far_real * far_real + far_imag * far_imag - intensity.astype(jnp.float32)
    pull_real = (misfit * far_real).astype(jnp.bfloat16)
    pull_imag = (misfit * far_imag).astype(jnp.bfloat16)
    back_real, back_imag = transform(pull_real, pull_imag, -1.0, cosine_table, sine_table)
    grad2_real, grad2_imag = to_half(complex_product(passed_real, -passed_imag, back_real, back_imag))
    inward_real, inward_imag = to_half(complex_product(second_real, -second_imag, back_real, back_imag))
    lifted_real, lifted_imag = transform(inward_real, inward_imag, 1.0, cosine_table, sine_table)
    reverted_real, reverted_imag = to_half(complex_product(spread_real, -spread_imag, lifted_real, lifted_imag))
    start_real, start_imag = transform(reverted_real, reverted_imag, -1.0, cosine_table, sine_table)
    grad1_real, grad1_imag = to_half(complex_product(light_real, -light_imag, start_real, start_imag))
    return jnp.stack([grad1_real, grad1_imag, grad2_real, grad2_imag], axis=1)

def reference(objects, illumination, propagator_phase, intensity, offsets, counts):
    margin = PROBE // 2
    cosine_table, sine_table = tables(PROBE)
    padded = jnp.pad(objects.astype(jnp.bfloat16), ((0, 0), (margin, margin), (margin, margin)))
    summed = jnp.zeros(padded.shape, jnp.float32)
    block_rows = math.gcd(SLOTS, 4)
    zero_index = jnp.zeros((), jnp.int32)

    def fetch(row_at, col_at):
        return lax.dynamic_slice(padded, (zero_index, row_at, col_at), (4, PROBE, PROBE))

    def one_block(block_id, summed):
        first = block_id.astype(jnp.int32) * block_rows
        number = first + jnp.arange(block_rows, dtype=jnp.int32)
        device = number // SLOTS
        slot_ids = number % SLOTS
        row_ids = device // N_COL
        col_ids = device % N_COL
        corners = lax.dynamic_slice_in_dim(offsets, first, block_rows, 0)
        start_row = (row_ids * TILE + (corners[:, 0] + 1) * margin).astype(jnp.int32)
        start_col = (col_ids * TILE + (corners[:, 1] + 1) * margin).astype(jnp.int32)
        live = slot_ids < counts[device]
        patches = jax.vmap(fetch)(start_row, start_col)
        measured = lax.dynamic_slice_in_dim(intensity, first, block_rows, 0)
        results = slot_gradient(illumination, propagator_phase, patches, measured, cosine_table, sine_table)
        results = jnp.where(live[:, None, None, None], results.astype(jnp.float32), jnp.zeros((), jnp.float32))
        for member in range(block_rows):
            where_at = (zero_index, start_row[member], start_col[member])
            window = lax.dynamic_slice(summed, where_at, (4, PROBE, PROBE))
            summed = lax.dynamic_update_slice(summed, window + results[member], where_at)
        return summed
    summed = lax.fori_loop(0, TASKS // block_rows, one_block, summed)
    return summed[:, margin:-margin, margin:-margin]
```

```python
import functools
import math

import jax
import jax.numpy as jnp
import numpy as np
from jax import lax
from jax.experimental import pallas as pl
from jax.experimental.pallas import tpu as pltpu
from jax.sharding import PartitionSpec as P

HALF = jnp.bfloat16
FULL = jnp.float32


def from_behind(x, axis, by):
    size = lax.axis_size(axis)
    pairs = [(i, i + by) for i in range(size) if 0 <= i + by < size]
    return lax.ppermute(x, axis, pairs)


def half_tables(extent):
    half = extent // 2
    number = np.arange(extent, dtype=np.int64)
    turns = (number[:, None] * number[None, :]) % extent
    angle = turns.astype(np.float32) * np.float32(2.0 * math.pi / extent)
    scale = np.float32(1.0 / math.sqrt(extent))
    cosine, sine = np.cos(angle) * scale, np.sin(angle) * scale
    tables = []
    for parity in range(2):
        c, s = cosine[parity::2, :half], sine[parity::2, :half]
        block = np.block([[c, s], [-s, c]])
        tables += [block, block.T]
    pick = np.zeros((extent, extent), np.float32)
    pick[number, np.concatenate([number[0::2], number[1::2]])] = 1.0
    tables += [pick, pick.T]
    return np.stack(tables).astype(HALF)


EVEN, EVEN_T, ODD, ODD_T, PICK, PICK_T = range(6)


def dot(left, right):
    return jnp.dot(left, right, preferred_element_type=FULL)


def beside(*parts):
    return jnp.concatenate(parts, axis=1)


def above(*parts):
    return jnp.concatenate(parts, axis=0)


def butterfly(x, n):
    top, bottom = x[:n] + x[n:], x[:n] - x[n:]
    return [
        beside(y[:, :n] + y[:, n:], y[:, :n] - y[:, n:]).astype(HALF) for y in (top, bottom)
    ]


def paired(first, second, side, n):
    cols = slice(side * n, side * n + n)
    return above(
        beside(first[:n, cols], first[n:, cols]), beside(second[:n, cols], second[n:, cols])
    )


def forward(real, imag, tab, n):
    even_real, odd_real = butterfly(real, n)
    even_imag, odd_imag = butterfly(imag, n)
    yield
    even = dot(tab[EVEN], above(even_real, even_imag)).astype(HALF)
    odd = dot(tab[ODD], above(odd_real, odd_imag)).astype(HALF)
    result = (
        dot(paired(even, odd, 0, n), tab[EVEN_T]),
        dot(paired(even, odd, 1, n), tab[ODD_T]),
    )
    yield
    return result


def inverse(even_cols, odd_cols, tab, n):
    yield

    def left(rows, table):
        stacked = above(
            beside(even_cols[rows, :n], odd_cols[rows, :n]),
            beside(even_cols[rows, n:], odd_cols[rows, n:]),
        )
        return dot(tab[table], stacked).astype(HALF)

    first, second = left(slice(0, n), EVEN_T), left(slice(n, 2 * n), ODD_T)
    even = dot(paired(first, second, 0, n), tab[EVEN])
    odd = dot(paired(first, second, 1, n), tab[ODD])
    yield
    low, high = [above(y[:n] + y[n:], y[:n] - y[n:]) for y in (even + odd, even - odd)]
    return beside(low[:, :n], high[:, :n]), beside(low[:, n:], high[:, n:])


def slot_steps(light, spread, plane, measured, tab, put, n):
    def turned(y, col, sign):
        h_real, h_imag = spread(0, col), sign * spread(1, col)
        real, imag = y[:, :n], y[:, n:]
        return beside(
            (h_real * real - h_imag * imag).astype(HALF),
            (h_real * imag + h_imag * real).astype(HALF),
        )

    def pull(y, level):
        real, imag = y[:, :n], y[:, n:]
        misfit = real * real + imag * imag - level
        return beside((misfit * real).astype(HALF), (misfit * imag).astype(HALF))

    p_real, p_imag = light(0), light(1)
    o_real, o_imag = plane(0), plane(1)
    even, odd = yield from forward(
        p_real * o_real - p_imag * o_imag, p_real * o_imag + p_imag * o_real, tab, n
    )
    passed_real, passed_imag = yield from inverse(turned(even, 0, 1.0), turned(odd, n, 1.0), tab, n)
    o_real, o_imag = plane(2), plane(3)
    even, odd = yield from forward(
        passed_real * o_real - passed_imag * o_imag,
        passed_real * o_imag + passed_imag * o_real,
        tab,
        n,
    )
    level = dot(dot(tab[PICK], measured()).astype(HALF), tab[PICK_T])
    back_real, back_imag = yield from inverse(
        pull(even, level[:, :n]), pull(odd, level[:, n:]), tab, n
    )
    put(2, passed_real * back_real + passed_imag * back_imag)
    put(3, passed_real * back_imag - passed_imag * back_real)
    o_real, o_imag = plane(2), plane(3)
    even, odd = yield from forward(
        o_real * back_real + o_imag * back_imag, o_real * back_imag - o_imag * back_real, tab, n
    )
    start_real, start_imag = yield from inverse(
        turned(even, 0, -1.0), turned(odd, n, -1.0), tab, n
    )
    p_real, p_imag = light(0), light(1)
    put(0, p_real * start_real + p_imag * start_imag)
    put(1, p_real * start_imag - p_imag * start_real)


def alternate(generators):
    waiting = list(generators)
    while waiting:
        waiting = [g for g in waiting if next(g, waiting) is not waiting]


def slots_kernel(late, extent, tile, *refs):
    n = extent // 2
    offsets, counts, refs = refs[0], refs[1], refs[2:]
    sources, refs = refs[: 7 if late else 3], refs[7 if late else 3 :]
    tab_hbm, light_hbm, spread_hbm, measured_hbm, refs = *refs[:4], refs[4:]
    if late:
        prior, refs = refs[0], refs[1:]
        outs, refs = refs[:7], refs[7:]
    else:
        outs, refs = refs[:1], refs[1:]
    window, total, tab, light, spread, measured, order, sems, *staging = refs
    slot_count = measured.shape[0]

    top = n if late else 0
    mid, inner = pl.ds(top, tile), pl.ds(n, tile)
    first, last = pl.ds(0, n), pl.ds(n + tile, n)
    moves = [
        (sources[0], window.at[:, mid, inner]),
        (sources[1], window.at[:, mid, first]),
        (sources[2], window.at[:, mid, last]),
    ]
    if late:
        moves += [
            (sources[3], window.at[:, first, inner]),
            (sources[4], window.at[:, last, inner]),
            (sources[5].at[:, pl.ds(0, n)], window.at[:, first, first]),
            (sources[5].at[:, pl.ds(n, n)], window.at[:, last, first]),
            (sources[6].at[:, pl.ds(0, n)], window.at[:, first, last]),
            (sources[6].at[:, pl.ds(n, n)], window.at[:, last, last]),
        ]
    moves += [(light_hbm, light), (tab_hbm, tab), (spread_hbm, spread), (measured_hbm, measured)]
    if late:
        moves += [(prior, total.at[:, mid])]
    copies = [
        pltpu.make_async_copy(source, target, sems.at[i])
        for i, (source, target) in enumerate(moves)
    ]
    for copy in copies:
        copy.start()

    rows = total.shape[1]

    def clear(at, count):
        def step(i, carry):
            total[:, pl.ds(pl.multiple_of(at + 32 * i, 32), 32)] = jnp.zeros(
                (4, 32, total.shape[2]), FULL
            )
            return carry

        lax.fori_loop(0, count // 32, step, 0)

    if late:
        clear(0, n)
        clear(n + tile, n)
    else:
        clear(0, rows)

    def choose(j, found):
        row = offsets[j, 0]
        inside = (row >= 0) & ((row + 2) * n <= tile)
        wanted = (j < counts[0]) & (jnp.logical_not(inside) if late else inside)

        @pl.when(wanted)
        def _():
            order[found] = j

        return found + wanted.astype(jnp.int32)

    found = lax.fori_loop(0, slot_count, choose, jnp.int32(0))
    for copy in copies:
        copy.wait()

    def steps(at):
        slot = order[at]
        row = pl.multiple_of(offsets[slot, 0] * n + top, n)
        col = pl.multiple_of((offsets[slot, 1] + 1) * n, n)
        here = (pl.ds(row, extent), pl.ds(col, extent))

        def put(k, value):
            total[(k, *here)] += value

        return slot_steps(
            lambda k: light[k],
            lambda k, at: spread[k, :, at : at + n],
            lambda k: window[(k, *here)].astype(FULL),
            lambda: measured[slot],
            tab,
            put,
            n,
        )

    def two(i, carry):
        alternate([steps(2 * i), steps(2 * i + 1)])
        return carry

    lax.fori_loop(0, found // 2, two, 0)

    @pl.when(found % 2 == 1)
    def _():
        alternate([steps(found - 1)])

    if late:
        side, corner = staging
        for k in range(4):
            for i, cols in enumerate((first, last)):
                side[i, k] = total[k, mid, cols].astype(HALF)
                corner[i, k] = above(total[k, first, cols], total[k, last, cols]).astype(HALF)
        moves = [
            (corner.at[0], outs[3]),
            (corner.at[1], outs[4]),
            (side.at[0], outs[1]),
            (side.at[1], outs[2]),
            (total.at[:, first, inner], outs[5]),
            (total.at[:, last, inner], outs[6]),
            (total.at[:, mid, inner], outs[0]),
        ]
    else:
        moves = [(total, outs[0])]
    copies = [
        pltpu.make_async_copy(source, target, sems.at[i])
        for i, (source, target) in enumerate(moves)
    ]
    for copy in copies:
        copy.start()
    for copy in copies:
        copy.wait()


def run_slots(late, offsets, counts, sources, tables, light, spread, measured, prior=None):
    slot_count, extent = measured.shape[:2]
    n = extent // 2
    tile = sources[0].shape[1]
    rows = tile + 2 * n if late else tile
    cols = tile + 2 * n
    if late:
        outs = [
            ((4, tile, tile), FULL),
            ((4, tile, n), HALF),
            ((4, tile, n), HALF),
            ((4, extent, n), HALF),
            ((4, extent, n), HALF),
            ((4, n, tile), FULL),
            ((4, n, tile), FULL),
        ]
    else:
        outs = [((4, rows, cols), FULL)]
    scratch = [
        pltpu.VMEM((4, rows, cols), HALF),
        pltpu.VMEM((4, rows, cols), FULL),
        pltpu.VMEM(tables.shape, HALF),
        pltpu.VMEM(light.shape, FULL),
        pltpu.VMEM(spread.shape, FULL),
        pltpu.VMEM(measured.shape, HALF),
        pltpu.SMEM((slot_count,), jnp.int32),
        pltpu.SemaphoreType.DMA((14,)),
    ]
    if late:
        scratch += [pltpu.VMEM((2, 4, tile, n), HALF), pltpu.VMEM((2, 4, extent, n), HALF)]
    anywhere = pl.BlockSpec(memory_space=pl.ANY)
    scalars = pl.BlockSpec(memory_space=pltpu.SMEM)
    operands = [*sources, tables, light, spread, measured] + ([prior] if late else [])
    flops = 48 * 2 * extent**3 // 2 * slot_count // 2
    return pl.pallas_call(
        functools.partial(slots_kernel, late, extent, tile),
        out_shape=[jax.ShapeDtypeStruct(*out) for out in outs],
        in_specs=[scalars, scalars] + [anywhere] * len(operands),
        out_specs=[anywhere] * len(outs),
        scratch_shapes=scratch,
        name="late_slots" if late else "early_slots",
        cost_estimate=pl.CostEstimate(flops=flops, bytes_accessed=16 << 20, transcendentals=0),
    )(offsets, counts, *operands)


def frequency_order(x):
    half = x.shape[0] // 2
    return x.reshape(half, 2, half, 2).transpose(1, 0, 3, 2).reshape(x.shape)


def per_device(objects, illumination, propagator_phase, intensity, offsets, counts):
    extent = intensity.shape[1]
    n = extent // 2
    tile_rows = objects.shape[1]
    top = objects[:, :n].astype(HALF)
    bottom = objects[:, -n:].astype(HALF)
    from_above = from_behind(bottom, "row", 1)
    from_below = from_behind(top, "row", -1)
    from_left = from_behind(objects[:, :, -n:].astype(HALF), "col", 1)
    from_right = from_behind(objects[:, :, :n].astype(HALF), "col", -1)
    rounded = objects.astype(HALF)
    phase = frequency_order(propagator_phase)
    spread = jnp.stack([jnp.cos(phase), jnp.sin(phase)])
    tables = jnp.asarray(half_tables(extent))
    shared = (tables, illumination, spread, intensity)
    (prior,) = run_slots(False, offsets, counts, [rounded, from_left, from_right], *shared)
    ends = [jnp.concatenate([from_above[:, :, c], from_below[:, :, c]], axis=1) for c in (slice(-n, None), slice(0, n))]
    corner_left = from_behind(ends[0], "col", 1)
    corner_right = from_behind(ends[1], "col", -1)
    sources = [rounded, from_left, from_right, from_above, from_below, corner_left, corner_right]
    center, side_left, side_right, end_left, end_right, band_top, band_bottom = run_slots(
        True, offsets, counts, sources, *shared, prior=prior
    )
    ends_from_right = from_behind(end_left, "col", -1).astype(FULL)
    ends_from_left = from_behind(end_right, "col", 1).astype(FULL)
    side_from_right = from_behind(side_left, "col", -1).astype(FULL)
    side_from_left = from_behind(side_right, "col", 1).astype(FULL)

    def whole(band, rows):
        band = band.at[:, :, -n:].add(ends_from_right[:, rows])
        return band.at[:, :, :n].add(ends_from_left[:, rows]).astype(HALF)

    band_from_below = from_behind(whole(band_top, slice(0, n)), "row", -1).astype(FULL)
    band_from_above = from_behind(whole(band_bottom, slice(n, None)), "row", 1).astype(FULL)
    center = center.at[:, :, -n:].add(side_from_right)
    center = center.at[:, :, :n].add(side_from_left)
    center = center.at[:, -n:].add(band_from_below)
    return center.at[:, :n].add(band_from_above)


def solution(mesh):
    placed = (
        P(None, "row", "col"),
        P(),
        P(),
        P(("row", "col"), None, None),
        P(("row", "col"), None),
        P(("row", "col")),
    )
    return jax.shard_map(
        per_device, mesh=mesh, in_specs=placed, out_specs=P(None, "row", "col"), check_vma=False
    )
```

```python
import functools
import math

import jax
import jax.numpy as jnp
import numpy as np
from jax import lax
from jax.experimental import pallas as pl
from jax.experimental.pallas import tpu as pltpu
from jax.sharding import PartitionSpec as P


HALF = jnp.bfloat16
FULL = jnp.float32


def from_behind(x, axis, by):
    size = lax.axis_size(axis)
    pairs = [(i, i + by) for i in range(size) if 0 <= i + by < size]
    return lax.ppermute(x, axis, pairs)


def half_tables(extent):
    half = extent // 2
    number = np.arange(extent, dtype=np.int64)
    turns = (number[:, None] * number[None, :]) % extent
    angle = turns.astype(np.float32) * np.float32(2.0 * math.pi / extent)
    scale = np.float32(1.0 / math.sqrt(extent))
    cosine, sine = np.cos(angle) * scale, np.sin(angle) * scale
    tables = []
    for parity in range(2):
        c, s = cosine[parity::2, :half], sine[parity::2, :half]
        block = np.block([[c, s], [-s, c]])
        tables += [block, block.T]
    pick = np.zeros((extent, extent), np.float32)
    pick[number, np.concatenate([number[0::2], number[1::2]])] = 1.0
    tables += [pick, pick.T]
    return np.stack(tables).astype(HALF)


EVEN, EVEN_T, ODD, ODD_T, PICK, PICK_T = range(6)


def dot(left, right):
    return jnp.dot(left, right, preferred_element_type=FULL)


def beside(*parts):
    return jnp.concatenate(parts, axis=1)


def above(*parts):
    return jnp.concatenate(parts, axis=0)


def butterfly(x, n):
    top, bottom = x[:n] + x[n:], x[:n] - x[n:]
    return [
        beside(y[:, :n] + y[:, n:], y[:, :n] - y[:, n:]).astype(HALF) for y in (top, bottom)
    ]


def paired(first, second, side, n):
    cols = slice(side * n, side * n + n)
    return above(
        beside(first[:n, cols], first[n:, cols]), beside(second[:n, cols], second[n:, cols])
    )


def forward(real, imag, tab, n):
    even_real, odd_real = butterfly(real, n)
    even_imag, odd_imag = butterfly(imag, n)
    yield
    even = dot(tab[EVEN], above(even_real, even_imag)).astype(HALF)
    odd = dot(tab[ODD], above(odd_real, odd_imag)).astype(HALF)
    result = (
        dot(paired(even, odd, 0, n), tab[EVEN_T]),
        dot(paired(even, odd, 1, n), tab[ODD_T]),
    )
    yield
    return result


def inverse(even_cols, odd_cols, tab, n):
    yield

    def left(rows, table):
        stacked = above(
            beside(even_cols[rows, :n], odd_cols[rows, :n]),
            beside(even_cols[rows, n:], odd_cols[rows, n:]),
        )
        return dot(tab[table], stacked).astype(HALF)

    first, second = left(slice(0, n), EVEN_T), left(slice(n, 2 * n), ODD_T)
    even = dot(paired(first, second, 0, n), tab[EVEN])
    odd = dot(paired(first, second, 1, n), tab[ODD])
    yield
    low, high = [above(y[:n] + y[n:], y[:n] - y[n:]) for y in (even + odd, even - odd)]
    return beside(low[:, :n], high[:, :n]), beside(low[:, n:], high[:, n:])


def slot_steps(light, spread, plane, measured, tab, put, n):
    def turned(y, col, sign):
        h_real, h_imag = spread(0, col), sign * spread(1, col)
        real, imag = y[:, :n], y[:, n:]
        return beside(
            (h_real * real - h_imag * imag).astype(HALF),
            (h_real * imag + h_imag * real).astype(HALF),
        )

    def pull(y, level):
        real, imag = y[:, :n], y[:, n:]
        misfit = real * real + imag * imag - level
        return beside((misfit * real).astype(HALF), (misfit * imag).astype(HALF))

    p_real, p_imag = light(0), light(1)
    o_real, o_imag = plane(0), plane(1)
    even, odd = yield from forward(
        p_real * o_real - p_imag * o_imag, p_real * o_imag + p_imag * o_real, tab, n
    )
    passed_real, passed_imag = yield from inverse(turned(even, 0, 1.0), turned(odd, n, 1.0), tab, n)
    o_real, o_imag = plane(2), plane(3)
    even, odd = yield from forward(
        passed_real * o_real - passed_imag * o_imag,
        passed_real * o_imag + passed_imag * o_real,
        tab,
        n,
    )
    level = dot(dot(tab[PICK], measured()).astype(HALF), tab[PICK_T])
    back_real, back_imag = yield from inverse(
        pull(even, level[:, :n]), pull(odd, level[:, n:]), tab, n
    )
    put(2, passed_real * back_real + passed_imag * back_imag)
    put(3, passed_real * back_imag - passed_imag * back_real)
    o_real, o_imag = plane(2), plane(3)
    even, odd = yield from forward(
        o_real * back_real + o_imag * back_imag, o_real * back_imag - o_imag * back_real, tab, n
    )
    start_real, start_imag = yield from inverse(
        turned(even, 0, -1.0), turned(odd, n, -1.0), tab, n
    )
    p_real, p_imag = light(0), light(1)
    put(0, p_real * start_real + p_imag * start_imag)
    put(1, p_real * start_imag - p_imag * start_real)


def alternate(generators):
    waiting = list(generators)
    while waiting:
        waiting = [g for g in waiting if next(g, waiting) is not waiting]


def selected(x, tab):
    result = None
    for _ in range(3):
        part = x.astype(HALF)
        x = x - part.astype(FULL)
        moved = dot(dot(tab[PICK], part).astype(HALF), tab[PICK_T])
        result = moved if result is None else result + moved
    return result


INSIDE, BESIDE, OVER, CORNER = range(4)
VMEM = pl.BlockSpec(memory_space=pltpu.VMEM)
SMEM = pl.BlockSpec(memory_space=pltpu.SMEM)
ANYWHERE = pl.BlockSpec(memory_space=pl.ANY)


def run_copies(moves, sems):
    copies = [
        pltpu.make_async_copy(source, target, sems.at[i])
        for i, (source, target) in enumerate(moves)
    ]
    for copy in copies:
        copy.start()
    for copy in copies:
        copy.wait()


def strips_kernel(first, last, top, bottom):
    top[...] = first[...].astype(HALF)
    bottom[...] = last[...].astype(HALF)


def strips(objects, n):
    planes, rows, cols = objects.shape
    block = (1, n, cols)
    out = jax.ShapeDtypeStruct((planes, n, cols), HALF)
    return pl.pallas_call(
        strips_kernel,
        grid=(planes,),
        in_specs=[
            pl.BlockSpec(block, lambda k: (k, 0, 0)),
            pl.BlockSpec(block, lambda k: (k, rows // n - 1, 0)),
        ],
        out_specs=[pl.BlockSpec(block, lambda k: (k, 0, 0))] * 2,
        out_shape=[out, out],
        compiler_params=pltpu.CompilerParams(vmem_limit_bytes=60 << 20),
        name="strips",
    )(objects, objects)


def prepare_kernel(n, objects, window, left, right):
    planes, tile = objects.shape[:2]
    for k in range(planes):
        plane = objects[k].astype(HALF)
        window[k, n : n + tile, n : n + tile] = plane
        left[k] = plane[:, :n]
        right[k] = plane[:, tile - n :]


def prepare(objects, n):
    planes, tile = objects.shape[:2]
    side = jax.ShapeDtypeStruct((planes, tile, n), HALF)
    return pl.pallas_call(
        functools.partial(prepare_kernel, n),
        in_specs=[VMEM],
        out_specs=[VMEM] * 3,
        out_shape=[
            jax.ShapeDtypeStruct((planes, tile + 2 * n, tile + 2 * n), HALF),
            side,
            side,
        ],
        compiler_params=pltpu.CompilerParams(vmem_limit_bytes=16 << 20),
        name="prepare",
    )(objects)


def slots_kernel(mode, offsets, counts, tab, light, spread, measured, *refs):
    order, sems = refs[-2:]
    slot_count, extent = measured.shape[:2]
    n = extent // 2
    if mode == INSIDE:
        window, total, spread_out = refs[:3]
    else:
        sources, (window, total), outs = refs[:2], refs[4:6], refs[6:-2]
    tile = window.shape[1] - 2 * n
    inner, first, last = pl.ds(n, tile), pl.ds(0, n), pl.ds(n + tile, n)

    if mode == INSIDE:

        def clear(i, carry):
            at = pl.ds(pl.multiple_of(32 * i, 32), 32)
            total[:, at] = jnp.zeros((4, 32, total.shape[2]), FULL)
            return carry

        lax.fori_loop(0, total.shape[1] // 32, clear, 0)
        phase = spread[...]
        spread_out[0] = selected(jnp.cos(phase), tab)
        spread_out[1] = selected(jnp.sin(phase), tab)
        spread = spread_out
    else:
        one, two = sources
        if mode == BESIDE:
            moves = [(one, (inner, first)), (two, (inner, last))]
        elif mode == OVER:
            moves = [(one, (first, inner)), (two, (last, inner))]
        else:
            moves = [
                (side.at[:, pl.ds(at, n)], (rows, cols))
                for side, cols in ((one, first), (two, last))
                for at, rows in ((0, first), (n, last))
            ]
        run_copies([(source, window.at[(slice(None), *at)]) for source, at in moves], sems)

    def within(at):
        return (at >= 0) & ((at + 2) * n <= tile)

    def choose(j, found):
        row_in, col_in = within(offsets[0, j]), within(offsets[1, j])
        wanted = j < counts[0]
        wanted &= row_in if mode in (INSIDE, BESIDE) else jnp.logical_not(row_in)
        wanted &= col_in if mode in (INSIDE, OVER) else jnp.logical_not(col_in)

        @pl.when(wanted)
        def _():
            order[found] = j

        return found + wanted.astype(jnp.int32)

    found = lax.fori_loop(0, slot_count, choose, jnp.int32(0))

    def steps(at):
        slot = order[at]
        row = pl.multiple_of((offsets[0, slot] + 1) * n, n)
        col = pl.multiple_of((offsets[1, slot] + 1) * n, n)
        here = (pl.ds(row, extent), pl.ds(col, extent))

        def put(k, value):
            total[(k, *here)] += value

        return slot_steps(
            lambda k: light[k],
            lambda k, at: spread[k, :, at : at + n],
            lambda k: window[(k, *here)].astype(FULL),
            lambda: measured[slot],
            tab,
            put,
            n,
        )

    def both(i, carry):
        alternate([steps(2 * i), steps(2 * i + 1)])
        return carry

    lax.fori_loop(0, found // 2, both, 0)

    @pl.when(found % 2 == 1)
    def _():
        alternate([steps(found - 1)])

    if mode == BESIDE:
        outs[0][...] = total[0, :8, :128]
    if mode == OVER:
        for k in range(4):
            for d, rows in enumerate((first, last)):
                outs[d][k] = total[k, rows, pl.ds(2 * n, tile - 2 * n)].astype(HALF)
    if mode == CORNER:
        ends, edge = outs[:2], outs[2]
        for k in range(4):
            for e, (cols, edge_cols) in enumerate(((first, pl.ds(n, n)), (last, pl.ds(tile, n)))):
                for d, rows in enumerate((first, last)):
                    ends[e][d, k] = total[k, rows, cols].astype(HALF)
                    edge[d, e, k] = total[k, rows, edge_cols]


def run_slots(mode, scalars, constants, window, total=None, sources=()):
    _, _, _, measured = constants
    slot_count, extent = measured.shape[:2]
    n = extent // 2
    tile = window.shape[1] - 2 * n
    square = (4, n, n)
    outs = {
        INSIDE: [(window.shape, FULL), ((2, extent, extent), FULL)],
        BESIDE: [((8, 128), FULL)],
        OVER: [((4, n, tile - 2 * n), HALF)] * 2,
        CORNER: [((2, *square), HALF)] * 2 + [((2, 2, *square), FULL)],
    }[mode]
    operands = [*scalars, *constants]
    specs = [SMEM, SMEM, VMEM, VMEM, VMEM, VMEM]
    aliases = {}
    if mode == INSIDE:
        operands += [window]
        specs += [VMEM]
    else:
        operands += [*sources, window, total]
        specs += [ANYWHERE, ANYWHERE, VMEM, VMEM]
        aliases = {8: 0, 9: 1}
        outs = [(window.shape, HALF), (total.shape, FULL)] + outs
    return pl.pallas_call(
        functools.partial(slots_kernel, mode),
        out_shape=[jax.ShapeDtypeStruct(*out) for out in outs],
        in_specs=specs,
        out_specs=[VMEM] * len(outs),
        scratch_shapes=[pltpu.SMEM((slot_count,), jnp.int32), pltpu.SemaphoreType.DMA((4,))],
        input_output_aliases=aliases,
        compiler_params=pltpu.CompilerParams(vmem_limit_bytes=24 << 20),
        cost_estimate=pl.CostEstimate(
            flops=3 * 52 * extent**3, bytes_accessed=0, transcendentals=0
        ),
    )(*operands)


def turn_kernel(n, over, below, token, to_left, to_right):
    tile = over.shape[2]
    for d, band in enumerate((over, below)):
        to_left[:, d * n : (d + 1) * n] = band[:, :, :n]
        to_right[:, d * n : (d + 1) * n] = band[:, :, tile - n :]


def turn(over, below, token):
    planes, n, _ = over.shape
    out = jax.ShapeDtypeStruct((planes, 2 * n, n), HALF)
    return pl.pallas_call(
        functools.partial(turn_kernel, n),
        out_shape=[out, out],
        in_specs=[VMEM] * 3,
        out_specs=[VMEM] * 2,
        compiler_params=pltpu.CompilerParams(vmem_limit_bytes=8 << 20),
        name="turn",
    )(over, below, token)


def sides_kernel(n, total, token, left, right):
    tile = left.shape[1]
    for k in range(left.shape[0]):
        left[k] = total[k, pl.ds(n, tile), pl.ds(0, n)].astype(HALF)
        right[k] = total[k, pl.ds(n, tile), pl.ds(n + tile, n)].astype(HALF)


def sides(total, token, n):
    out = jax.ShapeDtypeStruct((total.shape[0], total.shape[1] - 2 * n, n), HALF)
    return pl.pallas_call(
        functools.partial(sides_kernel, n),
        out_shape=[out, out],
        in_specs=[VMEM] * 2,
        out_specs=[VMEM] * 2,
        compiler_params=pltpu.CompilerParams(vmem_limit_bytes=8 << 20),
        name="sides",
    )(total, token)


def join_kernel(edge, from_left, from_right, up, down):
    for d, out in enumerate((up, down)):
        out[0] = (edge[d, 0] + from_left[d].astype(FULL)).astype(HALF)
        out[1] = (edge[d, 1] + from_right[d].astype(FULL)).astype(HALF)


def join(edge, from_left, from_right):
    out = jax.ShapeDtypeStruct(edge.shape[1:], HALF)
    return pl.pallas_call(
        join_kernel,
        out_shape=[out, out],
        in_specs=[VMEM] * 3,
        out_specs=[VMEM] * 2,
        compiler_params=pltpu.CompilerParams(vmem_limit_bytes=8 << 20),
        name="join",
    )(edge, from_left, from_right)


def settle_kernel(n, from_left, from_right, total_in, total, out, sems):
    tile = out.shape[1]
    inner = pl.ds(n, tile)
    for k in range(4):
        total[k, inner, pl.ds(n, n)] += from_left[k].astype(FULL)
        total[k, inner, pl.ds(tile, n)] += from_right[k].astype(FULL)
    rows = tile - 2 * n
    run_copies([(total.at[:, pl.ds(2 * n, rows), inner], out.at[:, pl.ds(n, rows)])], sems)


def settle(total, from_left, from_right, n):
    planes, tile = from_left.shape[:2]
    return pl.pallas_call(
        functools.partial(settle_kernel, n),
        out_shape=[
            jax.ShapeDtypeStruct(total.shape, FULL),
            jax.ShapeDtypeStruct((planes, tile, tile), FULL),
        ],
        in_specs=[VMEM] * 3,
        out_specs=[VMEM, ANYWHERE],
        scratch_shapes=[pltpu.SemaphoreType.DMA((1,))],
        input_output_aliases={2: 0},
        compiler_params=pltpu.CompilerParams(vmem_limit_bytes=16 << 20),
        name="settle",
    )(from_left, from_right, total)


def finish_kernel(n, core_over, core_below, edge_over, edge_below, total, out_in, out, band, sems):
    tile = out.shape[1]
    copies = []
    for d, (core, edge, at, to) in enumerate(
        ((core_over, edge_over, n, 0), (core_below, edge_below, tile, tile - n))
    ):
        rows = pl.ds(at, n)
        for k in range(4):
            band[d, k, :, :n] = total[k, rows, pl.ds(n, n)] + edge[0, k].astype(FULL)
            band[d, k, :, n : tile - n] = total[k, rows, pl.ds(2 * n, tile - 2 * n)] + core[
                k
            ].astype(FULL)
            band[d, k, :, tile - n :] = total[k, rows, pl.ds(tile, n)] + edge[1, k].astype(FULL)
        copies.append(pltpu.make_async_copy(band.at[d], out.at[:, pl.ds(to, n)], sems.at[d]))
        copies[-1].start()
    for copy in copies:
        copy.wait()


def finish(total, out, cores, edges, n):
    planes, tile = out.shape[:2]
    return pl.pallas_call(
        functools.partial(finish_kernel, n),
        out_shape=jax.ShapeDtypeStruct(out.shape, FULL),
        in_specs=[VMEM] * 5 + [ANYWHERE],
        out_specs=ANYWHERE,
        scratch_shapes=[pltpu.VMEM((2, planes, n, tile), FULL), pltpu.SemaphoreType.DMA((2,))],
        input_output_aliases={5: 0},
        compiler_params=pltpu.CompilerParams(vmem_limit_bytes=16 << 20),
        name="finish",
    )(*cores, *edges, total, out)


def per_device(objects, illumination, propagator_phase, intensity, offsets, counts):
    extent = intensity.shape[1]
    n = extent // 2
    scalars = (offsets.T, counts)
    top, bottom = strips(objects, n)
    from_above = from_behind(bottom, "row", 1)
    from_below = from_behind(top, "row", -1)
    window, left, right = prepare(objects, n)
    from_left = from_behind(right, "col", 1)
    from_right = from_behind(left, "col", -1)
    constants = [jnp.asarray(half_tables(extent)), illumination, propagator_phase, intensity]
    total, constants[2] = run_slots(INSIDE, scalars, constants, window)
    window, total, token = run_slots(
        BESIDE, scalars, constants, window, total, (from_left, from_right)
    )
    to_left, to_right = turn(from_above, from_below, token)
    corner_left = from_behind(to_right, "col", 1)
    corner_right = from_behind(to_left, "col", -1)
    window, total, core_up, core_down = run_slots(
        OVER, scalars, constants, window, total, (from_above, from_below)
    )
    core_below = from_behind(core_up, "row", -1)
    core_over = from_behind(core_down, "row", 1)
    _, total, ends_left, ends_right, edge = run_slots(
        CORNER, scalars, constants, window, total, (corner_left, corner_right)
    )
    ends_from_right = from_behind(ends_left, "col", -1)
    ends_from_left = from_behind(ends_right, "col", 1)
    edge_up, edge_down = join(edge, ends_from_left, ends_from_right)
    edge_below = from_behind(edge_up, "row", -1)
    edge_over = from_behind(edge_down, "row", 1)
    side_left, side_right = sides(total, edge_up, n)
    side_from_right = from_behind(side_left, "col", -1)
    side_from_left = from_behind(side_right, "col", 1)
    total, out = settle(total, side_from_left, side_from_right, n)
    return finish(total, out, (core_over, core_below), (edge_over, edge_below), n)


def solution(mesh):
    placed = (
        P(None, "row", "col"),
        P(),
        P(),
        P(("row", "col"), None, None),
        P(("row", "col"), None),
        P(("row", "col")),
    )
    return jax.shard_map(
        per_device, mesh=mesh, in_specs=placed, out_specs=P(None, "row", "col"), check_vma=False
    )
```

```python
import functools
import math

import jax
import jax.numpy as jnp
import numpy as np
from jax import lax
from jax.experimental import pallas as pl
from jax.experimental.pallas import tpu as pltpu
from jax.sharding import PartitionSpec as P


HALF = jnp.bfloat16
FULL = jnp.float32


def exchange(x, axis, turn):
    size = lax.axis_size(axis)
    pairs = [(i, i + 1) for i in range(turn, size - 1, 2)]
    return lax.ppermute(x, axis, pairs + [(j, i) for i, j in pairs])


def ahead(axis, turn):
    odd = lax.axis_index(axis) % 2
    return odd if turn == 0 else 1 - odd


def pick(side, low, high, size):
    return pl.ds(pl.multiple_of(high - side * (high - low), size), size)


def half_tables(extent):
    half = extent // 2
    number = np.arange(extent, dtype=np.int64)
    turns = (number[:, None] * number[None, :]) % extent
    angle = turns.astype(np.float32) * np.float32(2.0 * math.pi / extent)
    scale = np.float32(1.0 / math.sqrt(extent))
    cosine, sine = np.cos(angle) * scale, np.sin(angle) * scale
    tables = []
    for parity in range(2):
        c, s = cosine[parity::2, :half], sine[parity::2, :half]
        block = np.block([[c, s], [-s, c]])
        tables += [block, block.T]
    pick = np.zeros((extent, extent), np.float32)
    pick[number, np.concatenate([number[0::2], number[1::2]])] = 1.0
    tables += [pick, pick.T]
    return np.stack(tables).astype(HALF)


EVEN, EVEN_T, ODD, ODD_T, PICK, PICK_T = range(6)


def dot(left, right):
    return jnp.dot(left, right, preferred_element_type=FULL)


def beside(*parts):
    return jnp.concatenate(parts, axis=1)


def above(*parts):
    return jnp.concatenate(parts, axis=0)


def butterfly(x, n):
    top, bottom = x[:n] + x[n:], x[:n] - x[n:]
    return [
        beside(y[:, :n] + y[:, n:], y[:, :n] - y[:, n:]).astype(HALF) for y in (top, bottom)
    ]


def paired(first, second, side, n):
    cols = slice(side * n, side * n + n)
    return above(
        beside(first[:n, cols], first[n:, cols]), beside(second[:n, cols], second[n:, cols])
    )


def forward(real, imag, tab, n):
    even_real, odd_real = butterfly(real, n)
    even_imag, odd_imag = butterfly(imag, n)
    yield
    even = dot(tab[EVEN], above(even_real, even_imag)).astype(HALF)
    odd = dot(tab[ODD], above(odd_real, odd_imag)).astype(HALF)
    result = (
        dot(paired(even, odd, 0, n), tab[EVEN_T]),
        dot(paired(even, odd, 1, n), tab[ODD_T]),
    )
    yield
    return result


def inverse(even_cols, odd_cols, tab, n):
    yield

    def left(rows, table):
        stacked = above(
            beside(even_cols[rows, :n], odd_cols[rows, :n]),
            beside(even_cols[rows, n:], odd_cols[rows, n:]),
        )
        return dot(tab[table], stacked).astype(HALF)

    first, second = left(slice(0, n), EVEN_T), left(slice(n, 2 * n), ODD_T)
    even = dot(paired(first, second, 0, n), tab[EVEN])
    odd = dot(paired(first, second, 1, n), tab[ODD])
    yield
    low, high = [above(y[:n] + y[n:], y[:n] - y[n:]) for y in (even + odd, even - odd)]
    return beside(low[:, :n], high[:, :n]), beside(low[:, n:], high[:, n:])


def slot_steps(light, spread, plane, measured, tab, put, n):
    def turned(y, col, sign):
        h_real, h_imag = spread(0, col), sign * spread(1, col)
        real, imag = y[:, :n], y[:, n:]
        return beside(
            (h_real * real - h_imag * imag).astype(HALF),
            (h_real * imag + h_imag * real).astype(HALF),
        )

    def pull(y, level):
        real, imag = y[:, :n], y[:, n:]
        misfit = real * real + imag * imag - level
        return beside((misfit * real).astype(HALF), (misfit * imag).astype(HALF))

    p_real, p_imag = light(0), light(1)
    o_real, o_imag = plane(0), plane(1)
    even, odd = yield from forward(
        p_real * o_real - p_imag * o_imag, p_real * o_imag + p_imag * o_real, tab, n
    )
    passed_real, passed_imag = yield from inverse(turned(even, 0, 1.0), turned(odd, n, 1.0), tab, n)
    o_real, o_imag = plane(2), plane(3)
    even, odd = yield from forward(
        passed_real * o_real - passed_imag * o_imag,
        passed_real * o_imag + passed_imag * o_real,
        tab,
        n,
    )
    level = dot(dot(tab[PICK], measured()).astype(HALF), tab[PICK_T])
    back_real, back_imag = yield from inverse(
        pull(even, level[:, :n]), pull(odd, level[:, n:]), tab, n
    )
    put(2, passed_real * back_real + passed_imag * back_imag)
    put(3, passed_real * back_imag - passed_imag * back_real)
    o_real, o_imag = plane(2), plane(3)
    even, odd = yield from forward(
        o_real * back_real + o_imag * back_imag, o_real * back_imag - o_imag * back_real, tab, n
    )
    start_real, start_imag = yield from inverse(
        turned(even, 0, -1.0), turned(odd, n, -1.0), tab, n
    )
    p_real, p_imag = light(0), light(1)
    put(0, p_real * start_real + p_imag * start_imag)
    put(1, p_real * start_imag - p_imag * start_real)


def alternate(generators):
    waiting = list(generators)
    while waiting:
        waiting = [g for g in waiting if next(g, waiting) is not waiting]


def selected(x, tab):
    result = None
    for _ in range(3):
        part = x.astype(HALF)
        x = x - part.astype(FULL)
        moved = dot(dot(tab[PICK], part).astype(HALF), tab[PICK_T])
        result = moved if result is None else result + moved
    return result


INSIDE, BESIDE, OVER, CORNER = range(4)
VMEM = pl.BlockSpec(memory_space=pltpu.VMEM)
SMEM = pl.BlockSpec(memory_space=pltpu.SMEM)
ANYWHERE = pl.BlockSpec(memory_space=pl.ANY)


def run_copies(moves, sems):
    copies = [
        pltpu.make_async_copy(source, target, sems.at[i])
        for i, (source, target) in enumerate(moves)
    ]
    for copy in copies:
        copy.start()
    for copy in copies:
        copy.wait()


def prepare_kernel(n, objects, window, *strips):
    planes, tile = objects.shape[:2]
    for k in range(planes):
        window[k, n : n + tile, n : n + tile] = objects[k].astype(HALF)
    for turn in range(2):
        rows = pick(ahead("row", turn), 0, tile - n, n)
        cols = pick(ahead("col", turn), 0, tile - n, n)
        for k in range(planes):
            strips[turn][k] = objects[k, rows, :].astype(HALF)
            strips[2 + turn][k] = objects[k, :, cols].astype(HALF)


def prepare(objects, n):
    planes, tile = objects.shape[:2]
    flat = jax.ShapeDtypeStruct((planes, n, tile), HALF)
    tall = jax.ShapeDtypeStruct((planes, tile, n), HALF)
    whole = jax.ShapeDtypeStruct((planes, tile + 2 * n, tile + 2 * n), HALF)
    return pl.pallas_call(
        functools.partial(prepare_kernel, n),
        in_specs=[VMEM],
        out_specs=[VMEM] * 5,
        out_shape=[whole, flat, flat, tall, tall],
        compiler_params=pltpu.CompilerParams(vmem_limit_bytes=16 << 20),
        cost_estimate=pl.CostEstimate(
            flops=2000 * objects.size, bytes_accessed=6 * objects.size, transcendentals=0
        ),
        name="prepare",
    )(objects)


def slots_kernel(mode, offsets, counts, tab, light, spread, measured, *refs):
    order, sems = refs[-2:]
    slot_count, extent = measured.shape[:2]
    n = extent // 2
    if mode == INSIDE:
        window, total, spread_out = refs[:3]
    else:
        sources, (window, total), outs = refs[:2], refs[4:6], refs[6:-2]
    tile = window.shape[1] - 2 * n
    inner = pl.ds(n, tile)
    row_halo = [pick(ahead("row", turn), 0, n + tile, n) for turn in range(2)]
    col_halo = [pick(ahead("col", turn), 0, n + tile, n) for turn in range(2)]
    col_edge = [pick(ahead("col", turn), n, tile, n) for turn in range(2)]

    if mode == INSIDE:

        def clear(i, carry):
            at = pl.ds(pl.multiple_of(32 * i, 32), 32)
            total[:, at] = jnp.zeros((4, 32, total.shape[2]), FULL)
            return carry

        lax.fori_loop(0, total.shape[1] // 32, clear, 0)
        phase = spread[...]
        spread_out[0] = selected(jnp.cos(phase), tab)
        spread_out[1] = selected(jnp.sin(phase), tab)
        spread = spread_out
    else:
        if mode == BESIDE:
            moves = [(sources[turn], (inner, col_halo[turn])) for turn in range(2)]
        elif mode == OVER:
            moves = [(sources[turn], (row_halo[turn], inner)) for turn in range(2)]
        else:
            moves = [
                (sources[turn].at[d], (row_halo[d], col_halo[turn]))
                for turn in range(2)
                for d in range(2)
            ]
        run_copies([(source, window.at[(slice(None), *at)]) for source, at in moves], sems)

    def inside(at):
        return (at >= 0) & ((at + 2) * n <= tile)

    def listed(kind, found):
        def choose(j, found):
            row_in, col_in = inside(offsets[0, j]), inside(offsets[1, j])
            wanted = j < counts[0]
            wanted &= row_in if kind in (INSIDE, BESIDE) else jnp.logical_not(row_in)
            wanted &= col_in if kind in (INSIDE, OVER) else jnp.logical_not(col_in)

            @pl.when(wanted)
            def _():
                order[found] = j

            return found + wanted.astype(jnp.int32)

        return lax.fori_loop(0, slot_count, choose, found)

    found = jnp.int32(0)
    for kind in range(min(mode, OVER) if mode != CORNER else 0):
        found = listed(kind, found)
        odd = found % 2

        @pl.when(odd == 1)
        def _():
            order[0] = order[found - 1]

        found = odd
    found = listed(mode, found)

    def steps(at):
        slot = order[at]
        row = pl.multiple_of((offsets[0, slot] + 1) * n, n)
        col = pl.multiple_of((offsets[1, slot] + 1) * n, n)
        here = (pl.ds(row, extent), pl.ds(col, extent))

        def put(k, value):
            total[(k, *here)] += value

        return slot_steps(
            lambda k: light[k],
            lambda k, at: spread[k, :, at : at + n],
            lambda k: window[(k, *here)].astype(FULL),
            lambda: measured[slot],
            tab,
            put,
            n,
        )

    def both(i, carry):
        alternate([steps(2 * i), steps(2 * i + 1)])
        return carry

    lax.fori_loop(0, found // 2, both, 0)

    if mode in (OVER, CORNER):

        @pl.when(found % 2 == 1)
        def _():
            alternate([steps(found - 1)])

    if mode == BESIDE:
        outs[0][...] = total[0, :8, :128]
    if mode == OVER:
        for turn in range(2):
            for k in range(4):
                outs[turn][k] = total[k, row_halo[turn], pl.ds(2 * n, tile - 2 * n)].astype(HALF)
    if mode == CORNER:
        ends, edge = outs[:2], outs[2]
        for turn in range(2):
            for d in range(2):
                for k in range(4):
                    ends[turn][d, k] = total[k, row_halo[d], col_halo[turn]].astype(HALF)
                    edge[d, turn, k] = total[k, row_halo[d], col_edge[turn]]


def run_slots(mode, scalars, constants, window, total=None, sources=()):
    _, _, _, measured = constants
    slot_count, extent = measured.shape[:2]
    n = extent // 2
    tile = window.shape[1] - 2 * n
    square = (4, n, n)
    outs = {
        INSIDE: [(window.shape, FULL), ((2, extent, extent), FULL)],
        BESIDE: [((8, 128), FULL)],
        OVER: [((4, n, tile - 2 * n), HALF)] * 2,
        CORNER: [((2, *square), HALF)] * 2 + [((2, 2, *square), FULL)],
    }[mode]
    operands = [*scalars, *constants]
    specs = [SMEM, SMEM, VMEM, VMEM, VMEM, VMEM]
    aliases = {}
    if mode == INSIDE:
        operands += [window]
        specs += [VMEM]
    else:
        operands += [*sources, window, total]
        specs += [ANYWHERE, ANYWHERE, VMEM, VMEM]
        aliases = {8: 0, 9: 1}
        outs = [(window.shape, HALF), (total.shape, FULL)] + outs
    return pl.pallas_call(
        functools.partial(slots_kernel, mode),
        out_shape=[jax.ShapeDtypeStruct(*out) for out in outs],
        in_specs=specs,
        out_specs=[VMEM] * len(outs),
        scratch_shapes=[pltpu.SMEM((slot_count,), jnp.int32), pltpu.SemaphoreType.DMA((4,))],
        input_output_aliases=aliases,
        compiler_params=pltpu.CompilerParams(vmem_limit_bytes=24 << 20),
        cost_estimate=pl.CostEstimate(
            flops=3 * 52 * extent**3, bytes_accessed=0, transcendentals=0
        ),
    )(*operands)


def turn_kernel(n, first, second, token, *outs):
    planes, _, tile = first.shape
    for turn in range(2):
        cols = pick(ahead("col", turn), 0, tile - n, n)
        for d, band in enumerate((first, second)):
            for k in range(planes):
                outs[turn][d, k] = band[k, :, cols]


def turn_ends(first, second, token):
    planes, n, _ = first.shape
    out = jax.ShapeDtypeStruct((2, planes, n, n), HALF)
    return pl.pallas_call(
        functools.partial(turn_kernel, n),
        out_shape=[out, out],
        in_specs=[VMEM] * 3,
        out_specs=[VMEM] * 2,
        compiler_params=pltpu.CompilerParams(vmem_limit_bytes=8 << 20),
        name="turn",
    )(first, second, token)


def sides_kernel(n, total, token, *outs):
    planes, tile = outs[0].shape[:2]
    for turn in range(2):
        cols = pick(ahead("col", turn), 0, n + tile, n)
        for k in range(planes):
            outs[turn][k] = total[k, pl.ds(n, tile), cols].astype(HALF)


def sides(total, token, n):
    out = jax.ShapeDtypeStruct((total.shape[0], total.shape[1] - 2 * n, n), HALF)
    return pl.pallas_call(
        functools.partial(sides_kernel, n),
        out_shape=[out, out],
        in_specs=[VMEM] * 2,
        out_specs=[VMEM] * 2,
        compiler_params=pltpu.CompilerParams(vmem_limit_bytes=8 << 20),
        name="sides",
    )(total, token)


def join_kernel(edge, first, second, *outs):
    for d, out in enumerate(outs):
        out[0] = (edge[d, 0] + first[d].astype(FULL)).astype(HALF)
        out[1] = (edge[d, 1] + second[d].astype(FULL)).astype(HALF)


def join(edge, first, second):
    out = jax.ShapeDtypeStruct(edge.shape[1:], HALF)
    return pl.pallas_call(
        join_kernel,
        out_shape=[out, out],
        in_specs=[VMEM] * 3,
        out_specs=[VMEM] * 2,
        compiler_params=pltpu.CompilerParams(vmem_limit_bytes=8 << 20),
        name="join",
    )(edge, first, second)


def settle_kernel(n, first, second, total_in, total, out, sems):
    tile = out.shape[1]
    for turn, side in enumerate((first, second)):
        cols = pick(ahead("col", turn), n, tile, n)
        for k in range(out.shape[0]):
            total[k, pl.ds(n, tile), cols] += side[k].astype(FULL)
    rows = tile - 2 * n
    run_copies([(total.at[:, pl.ds(2 * n, rows), pl.ds(n, tile)], out.at[:, pl.ds(n, rows)])], sems)


def settle(total, first, second, n):
    planes, tile = first.shape[:2]
    return pl.pallas_call(
        functools.partial(settle_kernel, n),
        out_shape=[
            jax.ShapeDtypeStruct(total.shape, FULL),
            jax.ShapeDtypeStruct((planes, tile, tile), FULL),
        ],
        in_specs=[VMEM] * 3,
        out_specs=[VMEM, ANYWHERE],
        scratch_shapes=[pltpu.SemaphoreType.DMA((1,))],
        input_output_aliases={2: 0},
        compiler_params=pltpu.CompilerParams(vmem_limit_bytes=16 << 20),
        name="settle",
    )(first, second, total)


def finish_kernel(n, core_0, core_1, edge_0, edge_1, total, out_in, out, band, sems):
    planes, tile = out.shape[:2]
    copies = []
    for turn, (core, edge) in enumerate(((core_0, edge_0), (core_1, edge_1))):
        side = ahead("row", turn)
        rows = pick(side, n, tile, n)
        for k in range(planes):
            band[turn, k] = total[k, rows, pl.ds(n, tile)]
            band[turn, k, :, pl.ds(n, tile - 2 * n)] += core[k].astype(FULL)
            for e in range(2):
                band[turn, k, :, pick(ahead("col", e), 0, tile - n, n)] += edge[e, k].astype(FULL)
        target = out.at[:, pick(side, 0, tile - n, n)]
        copies.append(pltpu.make_async_copy(band.at[turn], target, sems.at[turn]))
        copies[-1].start()
    for copy in copies:
        copy.wait()


def finish(total, out, cores, edges, n):
    planes, tile = out.shape[:2]
    return pl.pallas_call(
        functools.partial(finish_kernel, n),
        out_shape=jax.ShapeDtypeStruct(out.shape, FULL),
        in_specs=[VMEM] * 5 + [ANYWHERE],
        out_specs=ANYWHERE,
        scratch_shapes=[pltpu.VMEM((2, planes, n, tile), FULL), pltpu.SemaphoreType.DMA((2,))],
        input_output_aliases={5: 0},
        compiler_params=pltpu.CompilerParams(vmem_limit_bytes=16 << 20),
        name="finish",
    )(*cores, *edges, total, out)


def both(parts, axis):
    return [exchange(part, axis, turn) for turn, part in enumerate(parts)]


def per_device(objects, illumination, propagator_phase, intensity, offsets, counts):
    extent = intensity.shape[1]
    n = extent // 2
    scalars = (offsets.T, counts)
    window, *strips = prepare(objects, n)
    over = both(strips[:2], "row")
    beside = both(strips[2:], "col")
    constants = [jnp.asarray(half_tables(extent)), illumination, propagator_phase, intensity]
    total, constants[2] = run_slots(INSIDE, scalars, constants, window)
    window, total, token = run_slots(BESIDE, scalars, constants, window, total, beside)
    corner = both(turn_ends(*over, token), "col")
    window, total, *cores = run_slots(OVER, scalars, constants, window, total, over)
    cores = both(cores, "row")
    _, total, *ends, edge = run_slots(CORNER, scalars, constants, window, total, corner)
    ends = both(ends, "col")
    joined = join(edge, *ends)
    edges = both(joined, "row")
    outer = both(sides(total, joined[0], n), "col")
    total, out = settle(total, *outer, n)
    return finish(total, out, cores, edges, n)


def solution(mesh):
    placed = (
        P(None, "row", "col"),
        P(),
        P(),
        P(("row", "col"), None, None),
        P(("row", "col"), None),
        P(("row", "col")),
    )
    return jax.shard_map(
        per_device, mesh=mesh, in_specs=placed, out_specs=P(None, "row", "col"), check_vma=False
    )
```

```python
import functools
import math

import jax
import jax.numpy as jnp
import numpy as np
from jax import lax
from jax.experimental import pallas as pl
from jax.experimental.pallas import tpu as pltpu
from jax.sharding import PartitionSpec as P


HALF = jnp.bfloat16
FULL = jnp.float32


def exchange(x, axis, turn):
    size = lax.axis_size(axis)
    pairs = [(i, i + 1) for i in range(turn, size - 1, 2)]
    return lax.ppermute(x, axis, pairs + [(j, i) for i, j in pairs])


def ahead(axis, turn):
    odd = lax.axis_index(axis) % 2
    return odd if turn == 0 else 1 - odd


def pick(side, low, high, size):
    return pl.ds(pl.multiple_of(high - side * (high - low), size), size)


def half_tables(extent):
    half = extent // 2
    number = np.arange(extent, dtype=np.int64)
    turns = (number[:, None] * number[None, :]) % extent
    angle = turns.astype(np.float32) * np.float32(2.0 * math.pi / extent)
    scale = np.float32(1.0 / math.sqrt(extent))
    cosine, sine = np.cos(angle) * scale, np.sin(angle) * scale
    tables = []
    for parity in range(2):
        c, s = cosine[parity::2, :half], sine[parity::2, :half]
        block = np.block([[c, s], [-s, c]])
        tables += [block, block.T]
    pick = np.zeros((extent, extent), np.float32)
    pick[number, np.concatenate([number[0::2], number[1::2]])] = 1.0
    tables += [pick, pick.T]
    return np.stack(tables).astype(HALF)


EVEN, EVEN_T, ODD, ODD_T, PICK, PICK_T = range(6)


def dot(left, right):
    return jnp.dot(left, right, preferred_element_type=FULL)


def beside(*parts):
    return jnp.concatenate(parts, axis=1)


def above(*parts):
    return jnp.concatenate(parts, axis=0)


def butterfly(x, n):
    top, bottom = x[:n] + x[n:], x[:n] - x[n:]
    return [
        beside(y[:, :n] + y[:, n:], y[:, :n] - y[:, n:]).astype(HALF) for y in (top, bottom)
    ]


def paired(first, second, side, n):
    cols = slice(side * n, side * n + n)
    return above(
        beside(first[:n, cols], first[n:, cols]), beside(second[:n, cols], second[n:, cols])
    )


def forward(real, imag, tab, n):
    even_real, odd_real = butterfly(real, n)
    even_imag, odd_imag = butterfly(imag, n)
    yield
    even = dot(tab[EVEN], above(even_real, even_imag)).astype(HALF)
    odd = dot(tab[ODD], above(odd_real, odd_imag)).astype(HALF)
    result = (
        dot(paired(even, odd, 0, n), tab[EVEN_T]),
        dot(paired(even, odd, 1, n), tab[ODD_T]),
    )
    yield
    return result


def inverse(even_cols, odd_cols, tab, n):
    yield

    def left(rows, table):
        stacked = above(
            beside(even_cols[rows, :n], odd_cols[rows, :n]),
            beside(even_cols[rows, n:], odd_cols[rows, n:]),
        )
        return dot(tab[table], stacked).astype(HALF)

    first, second = left(slice(0, n), EVEN_T), left(slice(n, 2 * n), ODD_T)
    even = dot(paired(first, second, 0, n), tab[EVEN])
    odd = dot(paired(first, second, 1, n), tab[ODD])
    yield
    low, high = [above(y[:n] + y[n:], y[:n] - y[n:]) for y in (even + odd, even - odd)]
    return beside(low[:, :n], high[:, :n]), beside(low[:, n:], high[:, n:])


def slot_steps(light, spread, plane, measured, tab, put, n):
    def turned(y, col, sign):
        h_real, h_imag = spread(0, col), sign * spread(1, col)
        real, imag = y[:, :n], y[:, n:]
        return beside(
            (h_real * real - h_imag * imag).astype(HALF),
            (h_real * imag + h_imag * real).astype(HALF),
        )

    def pull(y, level):
        real, imag = y[:, :n], y[:, n:]
        misfit = real * real + imag * imag - level
        return beside((misfit * real).astype(HALF), (misfit * imag).astype(HALF))

    p_real, p_imag = light(0), light(1)
    o_real, o_imag = plane(0), plane(1)
    even, odd = yield from forward(
        p_real * o_real - p_imag * o_imag, p_real * o_imag + p_imag * o_real, tab, n
    )
    passed_real, passed_imag = yield from inverse(turned(even, 0, 1.0), turned(odd, n, 1.0), tab, n)
    o_real, o_imag = plane(2), plane(3)
    even, odd = yield from forward(
        passed_real * o_real - passed_imag * o_imag,
        passed_real * o_imag + passed_imag * o_real,
        tab,
        n,
    )
    level = dot(dot(tab[PICK], measured()).astype(HALF), tab[PICK_T])
    back_real, back_imag = yield from inverse(
        pull(even, level[:, :n]), pull(odd, level[:, n:]), tab, n
    )
    put(2, passed_real * back_real + passed_imag * back_imag)
    put(3, passed_real * back_imag - passed_imag * back_real)
    o_real, o_imag = plane(2), plane(3)
    even, odd = yield from forward(
        o_real * back_real + o_imag * back_imag, o_real * back_imag - o_imag * back_real, tab, n
    )
    start_real, start_imag = yield from inverse(
        turned(even, 0, -1.0), turned(odd, n, -1.0), tab, n
    )
    p_real, p_imag = light(0), light(1)
    put(0, p_real * start_real + p_imag * start_imag)
    put(1, p_real * start_imag - p_imag * start_real)


def alternate(generators):
    waiting = list(generators)
    while waiting:
        waiting = [g for g in waiting if next(g, waiting) is not waiting]


def selected(x, tab):
    result = None
    for _ in range(3):
        part = x.astype(HALF)
        x = x - part.astype(FULL)
        moved = dot(dot(tab[PICK], part).astype(HALF), tab[PICK_T])
        result = moved if result is None else result + moved
    return result


INSIDE, BESIDE, OVER, CORNER = range(4)
VMEM = pl.BlockSpec(memory_space=pltpu.VMEM)
SMEM = pl.BlockSpec(memory_space=pltpu.SMEM)
ANYWHERE = pl.BlockSpec(memory_space=pl.ANY)


def run_copies(moves, sems):
    copies = [
        pltpu.make_async_copy(source, target, sems.at[i])
        for i, (source, target) in enumerate(moves)
    ]
    for copy in copies:
        copy.start()
    for copy in copies:
        copy.wait()


def prepare_kernel(n, objects, window, *strips):
    planes, tile = objects.shape[:2]
    for k in range(planes):
        window[k, n : n + tile, n : n + tile] = objects[k].astype(HALF)
    for turn in range(2):
        rows = pick(ahead("row", turn), 0, tile - n, n)
        cols = pick(ahead("col", turn), 0, tile - n, n)
        for k in range(planes):
            strips[turn][k] = objects[k, rows, :].astype(HALF)
            strips[2 + turn][k] = objects[k, :, cols].astype(HALF)


def prepare(objects, n):
    planes, tile = objects.shape[:2]
    flat = jax.ShapeDtypeStruct((planes, n, tile), HALF)
    tall = jax.ShapeDtypeStruct((planes, tile, n), HALF)
    whole = jax.ShapeDtypeStruct((planes, tile + 2 * n, tile + 2 * n), HALF)
    return pl.pallas_call(
        functools.partial(prepare_kernel, n),
        in_specs=[VMEM],
        out_specs=[VMEM] * 5,
        out_shape=[whole, flat, flat, tall, tall],
        compiler_params=pltpu.CompilerParams(vmem_limit_bytes=16 << 20),
        cost_estimate=pl.CostEstimate(
            flops=2000 * objects.size, bytes_accessed=6 * objects.size, transcendentals=0
        ),
        name="prepare",
    )(objects)


def slots_kernel(mode, offsets, counts, tab, light, spread, measured, *refs):
    order, sems = refs[-2:]
    slot_count, extent = measured.shape[:2]
    n = extent // 2
    if mode == INSIDE:
        window, total, spread_out = refs[:3]
    else:
        sources, (window, total), outs = refs[:2], refs[4:6], refs[6:-2]
    tile = window.shape[1] - 2 * n
    inner = pl.ds(n, tile)
    row_halo = [pick(ahead("row", turn), 0, n + tile, n) for turn in range(2)]
    col_halo = [pick(ahead("col", turn), 0, n + tile, n) for turn in range(2)]
    col_edge = [pick(ahead("col", turn), n, tile, n) for turn in range(2)]

    if mode == INSIDE:

        def clear(i, carry):
            at = pl.ds(pl.multiple_of(32 * i, 32), 32)
            total[:, at] = jnp.zeros((4, 32, total.shape[2]), FULL)
            return carry

        lax.fori_loop(0, total.shape[1] // 32, clear, 0)
        phase = spread[...]
        spread_out[0] = selected(jnp.cos(phase), tab)
        spread_out[1] = selected(jnp.sin(phase), tab)
        spread = spread_out
    else:
        if mode == BESIDE:
            moves = [(sources[turn], (inner, col_halo[turn])) for turn in range(2)]
        elif mode == OVER:
            moves = [(sources[turn], (row_halo[turn], inner)) for turn in range(2)]
        else:
            moves = [
                (sources[turn].at[d], (row_halo[d], col_halo[turn]))
                for turn in range(2)
                for d in range(2)
            ]
        run_copies([(source, window.at[(slice(None), *at)]) for source, at in moves], sems)

    def inside(at):
        return (at >= 0) & ((at + 2) * n <= tile)

    def listed(kind, found):
        def choose(j, found):
            row_in, col_in = inside(offsets[0, j]), inside(offsets[1, j])
            wanted = j < counts[0]
            wanted &= row_in if kind in (INSIDE, BESIDE) else jnp.logical_not(row_in)
            wanted &= col_in if kind in (INSIDE, OVER) else jnp.logical_not(col_in)

            @pl.when(wanted)
            def _():
                order[found] = j

            return found + wanted.astype(jnp.int32)

        return lax.fori_loop(0, slot_count, choose, found)

    found = jnp.int32(0)
    for kind in range(min(mode, OVER) if mode != CORNER else 0):
        found = listed(kind, found)
        odd = found % 2

        @pl.when(odd == 1)
        def _():
            order[0] = order[found - 1]

        found = odd
    found = listed(mode, found)

    def steps(at):
        slot = order[at]
        row = pl.multiple_of((offsets[0, slot] + 1) * n, n)
        col = pl.multiple_of((offsets[1, slot] + 1) * n, n)
        here = (pl.ds(row, extent), pl.ds(col, extent))

        def put(k, value):
            total[(k, *here)] += value

        return slot_steps(
            lambda k: light[k],
            lambda k, at: spread[k, :, at : at + n],
            lambda k: window[(k, *here)].astype(FULL),
            lambda: measured[slot],
            tab,
            put,
            n,
        )

    def both(i, carry):
        alternate([steps(2 * i), steps(2 * i + 1)])
        return carry

    lax.fori_loop(0, found // 2, both, 0)

    if mode in (OVER, CORNER):

        @pl.when(found % 2 == 1)
        def _():
            alternate([steps(found - 1)])

    if mode == BESIDE:
        outs[0][...] = total[0, :8, :128]
    if mode == OVER:
        for turn in range(2):
            for k in range(4):
                outs[turn][k] = total[k, row_halo[turn], pl.ds(2 * n, tile - 2 * n)].astype(HALF)
    if mode == CORNER:
        ends, edge = outs[:2], outs[2]
        for turn in range(2):
            for d in range(2):
                for k in range(4):
                    ends[turn][d, k] = total[k, row_halo[d], col_halo[turn]].astype(HALF)
                    edge[d, turn, k] = total[k, row_halo[d], col_edge[turn]]


def run_slots(mode, scalars, constants, window, total=None, sources=()):
    _, _, _, measured = constants
    slot_count, extent = measured.shape[:2]
    n = extent // 2
    tile = window.shape[1] - 2 * n
    square = (4, n, n)
    outs = {
        INSIDE: [(window.shape, FULL), ((2, extent, extent), FULL)],
        BESIDE: [((8, 128), FULL)],
        OVER: [((4, n, tile - 2 * n), HALF)] * 2,
        CORNER: [((2, *square), HALF)] * 2 + [((2, 2, *square), FULL)],
    }[mode]
    operands = [*scalars, *constants]
    specs = [SMEM, SMEM, VMEM, VMEM, VMEM, VMEM]
    aliases = {}
    if mode == INSIDE:
        operands += [window]
        specs += [VMEM]
    else:
        operands += [*sources, window, total]
        specs += [ANYWHERE, ANYWHERE, VMEM, VMEM]
        aliases = {8: 0, 9: 1}
        outs = [(window.shape, HALF), (total.shape, FULL)] + outs
    return pl.pallas_call(
        functools.partial(slots_kernel, mode),
        out_shape=[jax.ShapeDtypeStruct(*out) for out in outs],
        in_specs=specs,
        out_specs=[VMEM] * len(outs),
        scratch_shapes=[pltpu.SMEM((slot_count,), jnp.int32), pltpu.SemaphoreType.DMA((4,))],
        input_output_aliases=aliases,
        compiler_params=pltpu.CompilerParams(vmem_limit_bytes=24 << 20),
        cost_estimate=pl.CostEstimate(
            flops=3 * 52 * extent**3, bytes_accessed=0, transcendentals=0
        ),
    )(*operands)


def turn_kernel(n, first, second, token, *outs):
    planes, _, tile = first.shape
    for turn in range(2):
        cols = pick(ahead("col", turn), 0, tile - n, n)
        for d, band in enumerate((first, second)):
            for k in range(planes):
                outs[turn][d, k] = band[k, :, cols]


def turn_ends(first, second, token):
    planes, n, _ = first.shape
    out = jax.ShapeDtypeStruct((2, planes, n, n), HALF)
    return pl.pallas_call(
        functools.partial(turn_kernel, n),
        out_shape=[out, out],
        in_specs=[VMEM] * 3,
        out_specs=[VMEM] * 2,
        compiler_params=pltpu.CompilerParams(vmem_limit_bytes=8 << 20),
        name="turn",
    )(first, second, token)


def sides_kernel(n, total, *outs):
    planes, tile = outs[0].shape[:2]
    for turn in range(2):
        cols = pick(ahead("col", turn), 0, n + tile, n)
        for k in range(planes):
            outs[turn][k] = total[k, pl.ds(n, tile), cols].astype(HALF)


def sides(total, n):
    out = jax.ShapeDtypeStruct((total.shape[0], total.shape[1] - 2 * n, n), HALF)
    return pl.pallas_call(
        functools.partial(sides_kernel, n),
        out_shape=[out, out],
        in_specs=[VMEM],
        out_specs=[VMEM] * 2,
        compiler_params=pltpu.CompilerParams(vmem_limit_bytes=8 << 20),
        name="sides",
    )(total)


def join_kernel(edge, first, second, *outs):
    for d, out in enumerate(outs):
        out[0] = (edge[d, 0] + first[d].astype(FULL)).astype(HALF)
        out[1] = (edge[d, 1] + second[d].astype(FULL)).astype(HALF)


def join(edge, first, second):
    out = jax.ShapeDtypeStruct(edge.shape[1:], HALF)
    return pl.pallas_call(
        join_kernel,
        out_shape=[out, out],
        in_specs=[VMEM] * 3,
        out_specs=[VMEM] * 2,
        compiler_params=pltpu.CompilerParams(vmem_limit_bytes=8 << 20),
        name="join",
    )(edge, first, second)


def settle_kernel(n, first, second, total_in, total, out, sems):
    tile = out.shape[1]
    for turn, side in enumerate((first, second)):
        cols = pick(ahead("col", turn), n, tile, n)
        for k in range(out.shape[0]):
            total[k, pl.ds(n, tile), cols] += side[k].astype(FULL)
    rows = tile - 2 * n
    run_copies([(total.at[:, pl.ds(2 * n, rows), pl.ds(n, tile)], out.at[:, pl.ds(n, rows)])], sems)


def settle(total, first, second, n):
    planes, tile = first.shape[:2]
    return pl.pallas_call(
        functools.partial(settle_kernel, n),
        out_shape=[
            jax.ShapeDtypeStruct(total.shape, FULL),
            jax.ShapeDtypeStruct((planes, tile, tile), FULL),
        ],
        in_specs=[VMEM] * 3,
        out_specs=[VMEM, ANYWHERE],
        scratch_shapes=[pltpu.SemaphoreType.DMA((1,))],
        input_output_aliases={2: 0},
        compiler_params=pltpu.CompilerParams(vmem_limit_bytes=16 << 20),
        name="settle",
    )(first, second, total)


def finish_kernel(n, core_0, core_1, edge_0, edge_1, total, out_in, out, band, sems):
    planes, tile = out.shape[:2]
    copies = []
    for turn, (core, edge) in enumerate(((core_0, edge_0), (core_1, edge_1))):
        side = ahead("row", turn)
        rows = pick(side, n, tile, n)
        to = pick(side, 0, tile - n, n)
        for k in range(planes):
            band[turn, k, :, pl.ds(n, tile - 2 * n)] = total[
                k, rows, pl.ds(2 * n, tile - 2 * n)
            ] + core[k].astype(FULL)
            for e in range(2):
                at = ahead("col", e)
                band[turn, k, :, pick(at, 0, tile - n, n)] = total[
                    k, rows, pick(at, n, tile, n)
                ] + edge[e, k].astype(FULL)
            copies.append(
                pltpu.make_async_copy(
                    band.at[turn, k], out.at[k, to], sems.at[turn * planes + k]
                )
            )
            copies[-1].start()
    for copy in copies:
        copy.wait()


def finish(total, out, cores, edges, n):
    planes, tile = out.shape[:2]
    return pl.pallas_call(
        functools.partial(finish_kernel, n),
        out_shape=jax.ShapeDtypeStruct(out.shape, FULL),
        in_specs=[VMEM] * 5 + [ANYWHERE],
        out_specs=ANYWHERE,
        scratch_shapes=[
            pltpu.VMEM((2, planes, n, tile), FULL),
            pltpu.SemaphoreType.DMA((2 * planes,)),
        ],
        input_output_aliases={5: 0},
        compiler_params=pltpu.CompilerParams(vmem_limit_bytes=16 << 20),
        name="finish",
    )(*cores, *edges, total, out)


def both(parts, axis):
    return [exchange(part, axis, turn) for turn, part in enumerate(parts)]


def per_device(objects, illumination, propagator_phase, intensity, offsets, counts):
    extent = intensity.shape[1]
    n = extent // 2
    scalars = (offsets.T, counts)
    window, *strips = prepare(objects, n)
    over = both(strips[:2], "row")
    beside = both(strips[2:], "col")
    constants = [jnp.asarray(half_tables(extent)), illumination, propagator_phase, intensity]
    total, constants[2] = run_slots(INSIDE, scalars, constants, window)
    window, total, token = run_slots(BESIDE, scalars, constants, window, total, beside)
    corner = both(turn_ends(*over, token), "col")
    window, total, *cores = run_slots(OVER, scalars, constants, window, total, over)
    cores = both(cores, "row")
    _, total, *ends, edge = run_slots(CORNER, scalars, constants, window, total, corner)
    ends = both(ends, "col")
    outer = both(sides(total, n), "col")
    edges = both(join(edge, *ends), "row")
    total, out = settle(total, *outer, n)
    return finish(total, out, cores, edges, n)


def solution(mesh):
    placed = (
        P(None, "row", "col"),
        P(),
        P(),
        P(("row", "col"), None, None),
        P(("row", "col"), None),
        P(("row", "col")),
    )
    return jax.shard_map(
        per_device, mesh=mesh, in_specs=placed, out_specs=P(None, "row", "col"), check_vma=False
    )
```

```python
import functools
import math

import jax
import jax.numpy as jnp
import numpy as np
from jax import lax
from jax.experimental import pallas as pl
from jax.experimental.pallas import tpu as pltpu
from jax.sharding import PartitionSpec as P


HALF = jnp.bfloat16
FULL = jnp.float32


def exchange(x, axis, turn):
    size = lax.axis_size(axis)
    pairs = [(i, i + 1) for i in range(turn, size - 1, 2)]
    return lax.ppermute(x, axis, pairs + [(j, i) for i, j in pairs])


def ahead(axis, turn):
    odd = lax.axis_index(axis) % 2
    return odd if turn == 0 else 1 - odd


def pick(side, low, high, size):
    return pl.ds(pl.multiple_of(high - side * (high - low), size), size)


def half_tables(extent):
    half = extent // 2
    number = np.arange(extent, dtype=np.int64)
    turns = (number[:, None] * number[None, :]) % extent
    angle = turns.astype(np.float32) * np.float32(2.0 * math.pi / extent)
    scale = np.float32(1.0 / math.sqrt(extent))
    cosine, sine = np.cos(angle) * scale, np.sin(angle) * scale
    tables = []
    for parity in range(2):
        c, s = cosine[parity::2, :half], sine[parity::2, :half]
        block = np.block([[c, s], [-s, c]])
        tables += [block, block.T]
    pick = np.zeros((extent, extent), np.float32)
    pick[number, np.concatenate([number[0::2], number[1::2]])] = 1.0
    tables += [pick, pick.T]
    return np.stack(tables).astype(HALF)


EVEN, EVEN_T, ODD, ODD_T, PICK, PICK_T = range(6)


def dot(left, right):
    return jnp.dot(left, right, preferred_element_type=FULL)


def beside(*parts):
    return jnp.concatenate(parts, axis=1)


def above(*parts):
    return jnp.concatenate(parts, axis=0)


def stacked(fields, table):
    rows = fields[0].shape[0]
    result = dot(above(*fields) if len(fields) > 1 else fields[0], table)
    return [result[i * rows : (i + 1) * rows] for i in range(len(fields))]


def crossed(fields):
    return [x.astype(HALF).T for x in fields]


def paired(firsts, seconds, side, n):
    cols = slice(side * n, side * n + n)
    return [
        above(beside(x[:n, cols], x[n:, cols]), beside(y[:n, cols], y[n:, cols]))
        for x, y in zip(firsts, seconds)
    ]


def butterfly(x, n):
    y = above(x[:n] + x[n:], x[:n] - x[n:])
    return beside(y[:, :n] + y[:, n:], y[:, :n] - y[:, n:]).astype(HALF)


def forward(fields, tab, n):
    fields = [(butterfly(real, n), butterfly(imag, n)) for real, imag in fields]
    even = stacked([beside(r[:, :n], i[:, :n]) for r, i in fields], tab[EVEN_T])
    odd = stacked([beside(r[:, n:], i[:, n:]) for r, i in fields], tab[ODD_T])
    even, odd = crossed(even), crossed(odd)
    return (
        stacked(paired(even, odd, 0, n), tab[EVEN_T]),
        stacked(paired(even, odd, 1, n), tab[ODD_T]),
    )


def inverse(even, odd, tab, n):
    first = crossed(stacked(even, tab[EVEN]))
    second = crossed(stacked(odd, tab[ODD]))
    even = stacked(paired(first, second, 0, n), tab[EVEN])
    odd = stacked(paired(first, second, 1, n), tab[ODD])
    fields = []
    for x, y in zip(even, odd):
        low, high = [above(z[:n] + z[n:], z[:n] - z[n:]) for z in (x + y, x - y)]
        fields.append((beside(low[:, :n], high[:, :n]), beside(low[:, n:], high[:, n:])))
    return fields


def times(a, b):
    return a[0] * b[0] - a[1] * b[1], a[0] * b[1] + a[1] * b[0]


def times_conjugate(a, b):
    return a[0] * b[0] + a[1] * b[1], a[0] * b[1] - a[1] * b[0]


def slot_group(light, spread, planes, measured, tab, puts, n):
    def turned(fields, col, product):
        h = spread(col)
        pairs = [product(h, (y[:, :n], y[:, n:])) for y in fields]
        return [beside(real.astype(HALF), imag.astype(HALF)) for real, imag in pairs]

    def pull(fields, levels, col):
        results = []
        for y, level in zip(fields, levels):
            real, imag = y[:, :n], y[:, n:]
            misfit = real * real + imag * imag - level[:, col : col + n]
            results.append(beside((misfit * real).astype(HALF), (misfit * imag).astype(HALF)))
        return results

    even, odd = forward([times(light(), plane(0)) for plane in planes], tab, n)
    passed = inverse(turned(even, 0, times), turned(odd, n, times), tab, n)
    even, odd = forward([times(x, plane(2)) for x, plane in zip(passed, planes)], tab, n)
    levels = crossed(stacked([level() for level in measured], tab[PICK_T]))
    levels = stacked(levels, tab[PICK_T])
    back = inverse(pull(even, levels, 0), pull(odd, levels, n), tab, n)
    for put, x, y in zip(puts, passed, back):
        put(2, times_conjugate(x, y))
    even, odd = forward([times_conjugate(plane(2), y) for plane, y in zip(planes, back)], tab, n)
    start = inverse(
        turned(even, 0, times_conjugate), turned(odd, n, times_conjugate), tab, n
    )
    for put, y in zip(puts, start):
        put(0, times_conjugate(light(), y))


def wave_of(phase):
    half = phase * 0.5
    square = half * half
    sine, cosine = 0.0, 0.0
    for k in range(6, -1, -1):
        cosine = cosine * square + (-1.0) ** k / math.factorial(2 * k)
        sine = sine * square + (-1.0) ** k / math.factorial(2 * k + 1)
    sine = sine * half
    return 1.0 - 2.0 * sine * sine, 2.0 * sine * cosine


def selected(x, tab):
    result = None
    for _ in range(3):
        part = x.astype(HALF)
        x = x - part.astype(FULL)
        moved = dot(dot(tab[PICK], part).astype(HALF), tab[PICK_T])
        result = moved if result is None else result + moved
    return result


INSIDE, BESIDE, OVER, CORNER = range(4)
VMEM = pl.BlockSpec(memory_space=pltpu.VMEM)
SMEM = pl.BlockSpec(memory_space=pltpu.SMEM)
ANYWHERE = pl.BlockSpec(memory_space=pl.ANY)


def run_copies(moves, sems):
    copies = [
        pltpu.make_async_copy(source, target, sems.at[i])
        for i, (source, target) in enumerate(moves)
    ]
    for copy in copies:
        copy.start()
    for copy in copies:
        copy.wait()


def prepare_kernel(n, objects, window, *strips):
    planes, tile = objects.shape[:2]
    for k in range(planes):
        window[k, n : n + tile, n : n + tile] = objects[k].astype(HALF)
    for turn in range(2):
        rows = pick(ahead("row", turn), 0, tile - n, n)
        cols = pick(ahead("col", turn), 0, tile - n, n)
        for k in range(planes):
            strips[turn][k] = objects[k, rows, :].astype(HALF)
            strips[2 + turn][k] = objects[k, :, cols].astype(HALF)


def prepare(objects, n):
    planes, tile = objects.shape[:2]
    flat = jax.ShapeDtypeStruct((planes, n, tile), HALF)
    tall = jax.ShapeDtypeStruct((planes, tile, n), HALF)
    whole = jax.ShapeDtypeStruct((planes, tile + 2 * n, tile + 2 * n), HALF)
    return pl.pallas_call(
        functools.partial(prepare_kernel, n),
        in_specs=[VMEM],
        out_specs=[VMEM] * 5,
        out_shape=[whole, flat, flat, tall, tall],
        compiler_params=pltpu.CompilerParams(vmem_limit_bytes=16 << 20),
        cost_estimate=pl.CostEstimate(
            flops=2000 * objects.size, bytes_accessed=6 * objects.size, transcendentals=0
        ),
        name="prepare",
    )(objects)


def slots_kernel(mode, offsets, counts, tab, light, spread, measured, *refs):
    order = refs[-1]
    slot_count, extent = measured.shape[:2]
    n = extent // 2
    if mode == INSIDE:
        window, total, spread_out = refs[:3]
    else:
        sources, (window, total), outs = refs[:2], refs[4:6], refs[6:-1]
    tile = window.shape[1] - 2 * n
    inner = pl.ds(n, tile)
    row_halo = [pick(ahead("row", turn), 0, n + tile, n) for turn in range(2)]
    col_halo = [pick(ahead("col", turn), 0, n + tile, n) for turn in range(2)]
    col_edge = [pick(ahead("col", turn), n, tile, n) for turn in range(2)]

    if mode == INSIDE:

        def clear(i, carry):
            at = pl.ds(pl.multiple_of(32 * i, 32), 32)
            total[:, at] = jnp.zeros((4, 32, total.shape[2]), FULL)
            return carry

        lax.fori_loop(0, total.shape[1] // 32, clear, 0)
        for k, wave in enumerate(wave_of(spread[...].T)):
            spread_out[k] = selected(wave, tab)
        spread = spread_out
    else:
        if mode == BESIDE:
            moves = [(sources[turn], (inner, col_halo[turn])) for turn in range(2)]
        elif mode == OVER:
            moves = [(sources[turn], (row_halo[turn], inner)) for turn in range(2)]
        else:
            moves = [
                (sources[turn].at[d], (row_halo[d], col_halo[turn]))
                for turn in range(2)
                for d in range(2)
            ]
        for source, at in moves:
            for k in range(4):
                window[(k, *at)] = source[k]

    def inside(at):
        return (at >= 0) & ((at + 2) * n <= tile)

    def listed(kind, found):
        def choose(j, found):
            row_in, col_in = inside(offsets[0, j]), inside(offsets[1, j])
            wanted = j < counts[0]
            wanted &= row_in if kind in (INSIDE, BESIDE) else jnp.logical_not(row_in)
            wanted &= col_in if kind in (INSIDE, OVER) else jnp.logical_not(col_in)

            @pl.when(wanted)
            def _():
                order[found] = j

            return found + wanted.astype(jnp.int32)

        return lax.fori_loop(0, slot_count, choose, found)

    group = 2 if mode == CORNER else 3
    found = jnp.int32(0)
    for kind in range(mode if mode != CORNER else 0):
        found = listed(kind, found)
        left = found % group
        for i in range(group - 1):

            @pl.when(i < left)
            def _():
                order[i] = order[found - left + i]

        found = left
    found = listed(mode, found)

    def run(at, size):
        planes, puts, measures = [], [], []
        for i in range(size):
            slot = order[jnp.minimum(at + i, found - 1)]
            row = pl.multiple_of((offsets[0, slot] + 1) * n, n)
            col = pl.multiple_of((offsets[1, slot] + 1) * n, n)

            def plane(k, here=(pl.ds(row, extent), pl.ds(col, extent))):
                return window[(k, *here)].astype(FULL), window[(k + 1, *here)].astype(FULL)

            def put(k, pair, here=(pl.ds(row, extent), pl.ds(col, extent)), i=i):
                for part in range(2):
                    value = pair[part]
                    if mode == OVER and i == size - 1 and size > 1:
                        value = jnp.where(at + i < found, value, 0.0)
                    total[(k + part, *here)] += value

            planes.append(plane)
            puts.append(put)
            measures.append(lambda slot=slot: measured[slot])
        slot_group(
            lambda: (light[0], light[1]),
            lambda col: (spread[0, :, col : col + n], spread[1, :, col : col + n]),
            planes,
            measures,
            tab,
            puts,
            n,
        )

    def several(i, carry):
        run(group * i, group)
        return carry

    spare = 1 if mode == OVER else 0
    lax.fori_loop(0, (found + spare) // group, several, 0)
    if mode in (OVER, CORNER):

        @pl.when(found % group == 1)
        def _():
            run(found - 1, 1)

    if mode == BESIDE:
        outs[0][...] = total[0, :8, :128]
    if mode == OVER:
        for turn in range(2):
            for k in range(4):
                outs[turn][k] = total[k, row_halo[turn], pl.ds(2 * n, tile - 2 * n)].astype(HALF)
    if mode == CORNER:
        ends, edge = outs[:2], outs[2]
        for turn in range(2):
            for d in range(2):
                for k in range(4):
                    ends[turn][d, k] = total[k, row_halo[d], col_halo[turn]].astype(HALF)
                    edge[d, turn, k] = total[k, row_halo[d], col_edge[turn]]


def run_slots(mode, scalars, constants, window, total=None, sources=()):
    _, _, _, measured = constants
    slot_count, extent = measured.shape[:2]
    n = extent // 2
    tile = window.shape[1] - 2 * n
    square = (4, n, n)
    outs = {
        INSIDE: [(window.shape, FULL), ((2, extent, extent), FULL)],
        BESIDE: [((8, 128), FULL)],
        OVER: [((4, n, tile - 2 * n), HALF)] * 2,
        CORNER: [((2, *square), HALF)] * 2 + [((2, 2, *square), FULL)],
    }[mode]
    operands = [*scalars, *constants]
    specs = [SMEM, SMEM, VMEM, VMEM, VMEM, VMEM]
    aliases = {}
    if mode == INSIDE:
        operands += [window]
        specs += [VMEM]
    else:
        operands += [*sources, window, total]
        specs += [VMEM] * 4
        aliases = {8: 0, 9: 1}
        outs = [(window.shape, HALF), (total.shape, FULL)] + outs
    return pl.pallas_call(
        functools.partial(slots_kernel, mode),
        out_shape=[jax.ShapeDtypeStruct(*out) for out in outs],
        in_specs=specs,
        out_specs=[VMEM] * len(outs),
        scratch_shapes=[pltpu.SMEM((slot_count,), jnp.int32)],
        input_output_aliases=aliases,
        compiler_params=pltpu.CompilerParams(vmem_limit_bytes=24 << 20),
        cost_estimate=pl.CostEstimate(
            flops=3 * 52 * extent**3, bytes_accessed=0, transcendentals=0
        ),
    )(*operands)


def turn_kernel(n, first, second, token, *outs):
    planes, _, tile = first.shape
    for turn in range(2):
        cols = pick(ahead("col", turn), 0, tile - n, n)
        for d, band in enumerate((first, second)):
            for k in range(planes):
                outs[turn][d, k] = band[k, :, cols]


def turn_ends(first, second, token):
    planes, n, _ = first.shape
    out = jax.ShapeDtypeStruct((2, planes, n, n), HALF)
    return pl.pallas_call(
        functools.partial(turn_kernel, n),
        out_shape=[out, out],
        in_specs=[VMEM] * 3,
        out_specs=[VMEM] * 2,
        compiler_params=pltpu.CompilerParams(vmem_limit_bytes=8 << 20),
        name="turn",
    )(first, second, token)


def sides_kernel(n, total, *outs):
    planes, tile = outs[0].shape[:2]
    for turn in range(2):
        cols = pick(ahead("col", turn), 0, n + tile, n)
        for k in range(planes):
            outs[turn][k] = total[k, pl.ds(n, tile), cols].astype(HALF)


def sides(total, n):
    out = jax.ShapeDtypeStruct((total.shape[0], total.shape[1] - 2 * n, n), HALF)
    return pl.pallas_call(
        functools.partial(sides_kernel, n),
        out_shape=[out, out],
        in_specs=[VMEM],
        out_specs=[VMEM] * 2,
        compiler_params=pltpu.CompilerParams(vmem_limit_bytes=8 << 20),
        name="sides",
    )(total)


def join_kernel(edge, first, second, *outs):
    for d, out in enumerate(outs):
        out[0] = (edge[d, 0] + first[d].astype(FULL)).astype(HALF)
        out[1] = (edge[d, 1] + second[d].astype(FULL)).astype(HALF)


def join(edge, first, second):
    out = jax.ShapeDtypeStruct(edge.shape[1:], HALF)
    return pl.pallas_call(
        join_kernel,
        out_shape=[out, out],
        in_specs=[VMEM] * 3,
        out_specs=[VMEM] * 2,
        compiler_params=pltpu.CompilerParams(vmem_limit_bytes=8 << 20),
        name="join",
    )(edge, first, second)


def settle_kernel(n, first, second, total_in, total, out, sems):
    tile = out.shape[1]
    for turn, side in enumerate((first, second)):
        cols = pick(ahead("col", turn), n, tile, n)
        for k in range(out.shape[0]):
            total[k, pl.ds(n, tile), cols] += side[k].astype(FULL)
    rows = tile - 2 * n
    run_copies([(total.at[:, pl.ds(2 * n, rows), pl.ds(n, tile)], out.at[:, pl.ds(n, rows)])], sems)


def settle(total, first, second, n):
    planes, tile = first.shape[:2]
    return pl.pallas_call(
        functools.partial(settle_kernel, n),
        out_shape=[
            jax.ShapeDtypeStruct(total.shape, FULL),
            jax.ShapeDtypeStruct((planes, tile, tile), FULL),
        ],
        in_specs=[VMEM] * 3,
        out_specs=[VMEM, ANYWHERE],
        scratch_shapes=[pltpu.SemaphoreType.DMA((1,))],
        input_output_aliases={2: 0},
        compiler_params=pltpu.CompilerParams(vmem_limit_bytes=16 << 20),
        name="settle",
    )(first, second, total)


def finish_kernel(n, core_0, core_1, edge_0, edge_1, total, out_in, out, band, sems):
    planes, tile = out.shape[:2]
    copies = []
    for turn, (core, edge) in enumerate(((core_0, edge_0), (core_1, edge_1))):
        side = ahead("row", turn)
        rows = pick(side, n, tile, n)
        to = pick(side, 0, tile - n, n)
        for k in range(planes):
            band[turn, k, :, pl.ds(n, tile - 2 * n)] = total[
                k, rows, pl.ds(2 * n, tile - 2 * n)
            ] + core[k].astype(FULL)
            for e in range(2):
                at = ahead("col", e)
                band[turn, k, :, pick(at, 0, tile - n, n)] = total[
                    k, rows, pick(at, n, tile, n)
                ] + edge[e, k].astype(FULL)
            copies.append(
                pltpu.make_async_copy(
                    band.at[turn, k], out.at[k, to], sems.at[turn * planes + k]
                )
            )
            copies[-1].start()
    for copy in copies:
        copy.wait()


def finish(total, out, cores, edges, n):
    planes, tile = out.shape[:2]
    return pl.pallas_call(
        functools.partial(finish_kernel, n),
        out_shape=jax.ShapeDtypeStruct(out.shape, FULL),
        in_specs=[VMEM] * 5 + [ANYWHERE],
        out_specs=ANYWHERE,
        scratch_shapes=[
            pltpu.VMEM((2, planes, n, tile), FULL),
            pltpu.SemaphoreType.DMA((2 * planes,)),
        ],
        input_output_aliases={5: 0},
        compiler_params=pltpu.CompilerParams(vmem_limit_bytes=16 << 20),
        name="finish",
    )(*cores, *edges, total, out)


def both(parts, axis):
    return [exchange(part, axis, turn) for turn, part in enumerate(parts)]


def per_device(objects, illumination, propagator_phase, intensity, offsets, counts):
    extent = intensity.shape[1]
    n = extent // 2
    scalars = (offsets.T, counts)
    window, *strips = prepare(objects, n)
    over = both(strips[:2], "row")
    beside = both(strips[2:], "col")
    constants = [jnp.asarray(half_tables(extent)), illumination, propagator_phase, intensity]
    total, constants[2] = run_slots(INSIDE, scalars, constants, window)
    window, total, token = run_slots(BESIDE, scalars, constants, window, total, beside)
    corner = both(turn_ends(*over, token), "col")
    window, total, *cores = run_slots(OVER, scalars, constants, window, total, over)
    cores = both(cores, "row")
    _, total, *ends, edge = run_slots(CORNER, scalars, constants, window, total, corner)
    ends = both(ends, "col")
    outer = both(sides(total, n), "col")
    edges = both(join(edge, *ends), "row")
    total, out = settle(total, *outer, n)
    return finish(total, out, cores, edges, n)


def solution(mesh):
    placed = (
        P(None, "row", "col"),
        P(),
        P(),
        P(("row", "col"), None, None),
        P(("row", "col"), None),
        P(("row", "col")),
    )
    return jax.shard_map(
        per_device, mesh=mesh, in_specs=placed, out_specs=P(None, "row", "col"), check_vma=False
    )
```

```python
import functools
import math

import jax
import jax.numpy as jnp
import numpy as np
from jax import lax
from jax.experimental import pallas as pl
from jax.experimental.pallas import tpu as pltpu
from jax.sharding import PartitionSpec as P


HALF = jnp.bfloat16
FULL = jnp.float32


def exchange(x, axis, turn):
    size = lax.axis_size(axis)
    pairs = [(i, i + 1) for i in range(turn, size - 1, 2)]
    return lax.ppermute(x, axis, pairs + [(j, i) for i, j in pairs])


def ahead(axis, turn):
    odd = lax.axis_index(axis) % 2
    return odd if turn == 0 else 1 - odd


def pick(side, low, high, size):
    return pl.ds(pl.multiple_of(high - side * (high - low), size), size)


def half_tables(extent):
    half = extent // 2
    number = np.arange(extent, dtype=np.int64)
    turns = (number[:, None] * number[None, :]) % extent
    angle = turns.astype(np.float32) * np.float32(2.0 * math.pi / extent)
    scale = np.float32(1.0 / math.sqrt(extent))
    cosine, sine = np.cos(angle) * scale, np.sin(angle) * scale
    tables = []
    for parity in range(2):
        c, s = cosine[parity::2, :half], sine[parity::2, :half]
        block = np.block([[c, s], [-s, c]])
        tables += [block, block.T]
    pick = np.zeros((extent, extent), np.float32)
    pick[number, np.concatenate([number[0::2], number[1::2]])] = 1.0
    tables += [pick, pick.T]
    return np.stack(tables).astype(HALF)


EVEN, EVEN_T, ODD, ODD_T, PICK, PICK_T = range(6)


def dot(left, right):
    return jnp.dot(left, right, preferred_element_type=FULL)


def beside(*parts):
    return jnp.concatenate(parts, axis=1)


def above(*parts):
    return jnp.concatenate(parts, axis=0)


def stacked(fields, table):
    rows = fields[0].shape[0]
    result = dot(above(*fields) if len(fields) > 1 else fields[0], table)
    return [result[i * rows : (i + 1) * rows] for i in range(len(fields))]


def crossed(fields):
    return [x.astype(HALF).T for x in fields]


def paired(firsts, seconds, side, n):
    cols = slice(side * n, side * n + n)
    return [
        above(beside(x[:n, cols], x[n:, cols]), beside(y[:n, cols], y[n:, cols]))
        for x, y in zip(firsts, seconds)
    ]


def butterfly(x, n):
    y = above(x[:n] + x[n:], x[:n] - x[n:])
    return beside(y[:, :n] + y[:, n:], y[:, :n] - y[:, n:]).astype(HALF)


def forward(fields, tab, n):
    fields = [(butterfly(real, n), butterfly(imag, n)) for real, imag in fields]
    even = stacked([beside(r[:, :n], i[:, :n]) for r, i in fields], tab[EVEN_T])
    odd = stacked([beside(r[:, n:], i[:, n:]) for r, i in fields], tab[ODD_T])
    even, odd = crossed(even), crossed(odd)
    return (
        stacked(paired(even, odd, 0, n), tab[EVEN_T]),
        stacked(paired(even, odd, 1, n), tab[ODD_T]),
    )


def inverse(even, odd, tab, n):
    first = crossed(stacked(even, tab[EVEN]))
    second = crossed(stacked(odd, tab[ODD]))
    even = stacked(paired(first, second, 0, n), tab[EVEN])
    odd = stacked(paired(first, second, 1, n), tab[ODD])
    fields = []
    for x, y in zip(even, odd):
        low, high = [above(z[:n] + z[n:], z[:n] - z[n:]) for z in (x + y, x - y)]
        fields.append((beside(low[:, :n], high[:, :n]), beside(low[:, n:], high[:, n:])))
    return fields


def times(a, b):
    return a[0] * b[0] - a[1] * b[1], a[0] * b[1] + a[1] * b[0]


def times_conjugate(a, b):
    return a[0] * b[0] + a[1] * b[1], a[0] * b[1] - a[1] * b[0]


def slot_group(light, spread, planes, measured, tab, puts, n):
    def turned(fields, col, product):
        h = spread(col)
        pairs = [product(h, (y[:, :n], y[:, n:])) for y in fields]
        return [beside(real.astype(HALF), imag.astype(HALF)) for real, imag in pairs]

    def pull(fields, levels, col):
        results = []
        for y, level in zip(fields, levels):
            real, imag = y[:, :n], y[:, n:]
            misfit = real * real + imag * imag - level[:, col : col + n]
            results.append(beside((misfit * real).astype(HALF), (misfit * imag).astype(HALF)))
        return results

    even, odd = forward([times(light(), plane(0)) for plane in planes], tab, n)
    passed = inverse(turned(even, 0, times), turned(odd, n, times), tab, n)
    even, odd = forward([times(x, plane(2)) for x, plane in zip(passed, planes)], tab, n)
    levels = crossed(stacked([level() for level in measured], tab[PICK_T]))
    levels = stacked(levels, tab[PICK_T])
    back = inverse(pull(even, levels, 0), pull(odd, levels, n), tab, n)
    for put, x, y in zip(puts, passed, back):
        put(2, times_conjugate(x, y))
    even, odd = forward([times_conjugate(plane(2), y) for plane, y in zip(planes, back)], tab, n)
    start = inverse(
        turned(even, 0, times_conjugate), turned(odd, n, times_conjugate), tab, n
    )
    for put, y in zip(puts, start):
        put(0, times_conjugate(light(), y))


def wave_of(phase):
    half = phase * 0.5
    square = half * half
    sine, cosine = 0.0, 0.0
    for k in range(6, -1, -1):
        cosine = cosine * square + (-1.0) ** k / math.factorial(2 * k)
        sine = sine * square + (-1.0) ** k / math.factorial(2 * k + 1)
    sine = sine * half
    return 1.0 - 2.0 * sine * sine, 2.0 * sine * cosine


def selected(x, tab):
    result = None
    for _ in range(3):
        part = x.astype(HALF)
        x = x - part.astype(FULL)
        moved = dot(dot(tab[PICK], part).astype(HALF), tab[PICK_T])
        result = moved if result is None else result + moved
    return result


INSIDE, BESIDE, OVER, CORNER = range(4)
VMEM = pl.BlockSpec(memory_space=pltpu.VMEM)
SMEM = pl.BlockSpec(memory_space=pltpu.SMEM)
ANYWHERE = pl.BlockSpec(memory_space=pl.ANY)


def run_copies(moves, sems):
    copies = [
        pltpu.make_async_copy(source, target, sems.at[i])
        for i, (source, target) in enumerate(moves)
    ]
    for copy in copies:
        copy.start()
    for copy in copies:
        copy.wait()


def prepare_kernel(n, objects, window, *strips):
    planes, tile = objects.shape[:2]
    for k in range(planes):
        window[k, n : n + tile, n : n + tile] = objects[k].astype(HALF)
    for turn in range(2):
        rows = pick(ahead("row", turn), 0, tile - n, n)
        cols = pick(ahead("col", turn), 0, tile - n, n)
        for k in range(planes):
            strips[turn][k] = objects[k, rows, :].astype(HALF)
            strips[2 + turn][k] = objects[k, :, cols].astype(HALF)


def prepare(objects, n):
    planes, tile = objects.shape[:2]
    flat = jax.ShapeDtypeStruct((planes, n, tile), HALF)
    tall = jax.ShapeDtypeStruct((planes, tile, n), HALF)
    whole = jax.ShapeDtypeStruct((planes, tile + 2 * n, tile + 2 * n), HALF)
    return pl.pallas_call(
        functools.partial(prepare_kernel, n),
        in_specs=[VMEM],
        out_specs=[VMEM] * 5,
        out_shape=[whole, flat, flat, tall, tall],
        compiler_params=pltpu.CompilerParams(vmem_limit_bytes=16 << 20),
        cost_estimate=pl.CostEstimate(
            flops=2000 * objects.size, bytes_accessed=6 * objects.size, transcendentals=0
        ),
        name="prepare",
    )(objects)


def slots_kernel(mode, offsets, counts, tab, light, spread, measured, *refs):
    order = refs[-1]
    slot_count, extent = measured.shape[:2]
    n = extent // 2
    if mode == INSIDE:
        window, total, spread_out = refs[:3]
    else:
        m = {BESIDE: 3, OVER: 1, CORNER: 2}[mode]
        sources, (window, total), outs = refs[:m], refs[m + 2 : m + 4], refs[m + 4 : -1]
    tile = window.shape[1] - 2 * n
    inner = pl.ds(n, tile)
    row_halo = [pick(ahead("row", turn), 0, n + tile, n) for turn in range(2)]
    col_halo = [pick(ahead("col", turn), 0, n + tile, n) for turn in range(2)]
    col_edge = [pick(ahead("col", turn), n, tile, n) for turn in range(2)]

    if mode == INSIDE:

        def clear(i, carry):
            at = pl.ds(pl.multiple_of(32 * i, 32), 32)
            total[:, at] = jnp.zeros((4, 32, total.shape[2]), FULL)
            return carry

        lax.fori_loop(0, total.shape[1] // 32, clear, 0)
        for k, wave in enumerate(wave_of(spread[...].T)):
            spread_out[k] = selected(wave, tab)
        spread = spread_out
    else:
        if mode == BESIDE:
            moves = [(sources[turn], (inner, col_halo[turn])) for turn in range(2)]
            moves += [(sources[2], (row_halo[0], inner))]
        elif mode == OVER:
            moves = [(sources[0], (row_halo[1], inner))]
        else:
            moves = [
                (sources[turn].at[d], (row_halo[d], col_halo[turn]))
                for turn in range(2)
                for d in range(2)
            ]
        for source, at in moves:
            for k in range(4):
                window[(k, *at)] = source[k]

    def inside(at):
        return (at >= 0) & ((at + 2) * n <= tile)

    def listed(kind, found):
        for j in range(slot_count):
            row, col = offsets[0, j], offsets[1, j]
            early = inside(row) | ((row < 0) == (ahead("row", 0) == 1))
            wanted = j < counts[0]
            if kind == INSIDE:
                wanted &= inside(row) & inside(col)
            elif kind == BESIDE:
                wanted &= (inside(row) != inside(col)) & early
            elif kind == OVER:
                wanted &= jnp.logical_not(early) & inside(col)
            else:
                wanted &= jnp.logical_not(inside(row) | inside(col))
            order[found] = j
            found = found + wanted.astype(jnp.int32)
        return found

    group = 3 if mode in (INSIDE, BESIDE) else 2
    found = jnp.int32(0)
    if mode == BESIDE:
        found = listed(INSIDE, found)
        left = found % group
        for i in range(group - 1):
            order[i] = order[jnp.maximum(found - left + i, 0)]
        found = left
    found = listed(mode, found)

    def run(at, size):
        planes, puts, measures = [], [], []
        for i in range(size):
            slot = order[jnp.minimum(at + i, found - 1)]
            row = pl.multiple_of((offsets[0, slot] + 1) * n, n)
            col = pl.multiple_of((offsets[1, slot] + 1) * n, n)

            def plane(k, here=(pl.ds(row, extent), pl.ds(col, extent))):
                return window[(k, *here)].astype(FULL), window[(k + 1, *here)].astype(FULL)

            def put(k, pair, here=(pl.ds(row, extent), pl.ds(col, extent)), i=i):
                for part in range(2):
                    value = pair[part]
                    if mode == BESIDE and i == size - 1 and size > 1:
                        value = jnp.where(at + i < found, value, 0.0)
                    total[(k + part, *here)] += value

            planes.append(plane)
            puts.append(put)
            measures.append(lambda slot=slot: measured[slot])
        slot_group(
            lambda: (light[0], light[1]),
            lambda col: (spread[0, :, col : col + n], spread[1, :, col : col + n]),
            planes,
            measures,
            tab,
            puts,
            n,
        )

    def several(i, carry):
        run(group * i, group)
        return carry

    spare = 1 if mode == BESIDE else 0
    lax.fori_loop(0, (found + spare) // group, several, 0)
    if mode != INSIDE:

        @pl.when(found % group == 1)
        def _():
            run(found - 1, 1)

    if mode in (BESIDE, OVER):
        rows = row_halo[0 if mode == BESIDE else 1]
        for k in range(4):
            outs[0][k] = total[k, rows, pl.ds(2 * n, tile - 2 * n)].astype(HALF)
    if mode == CORNER:
        ends, edge = outs[:2], outs[2]
        for turn in range(2):
            for d in range(2):
                for k in range(4):
                    ends[turn][d, k] = total[k, row_halo[d], col_halo[turn]].astype(HALF)
                    edge[d, turn, k] = total[k, row_halo[d], col_edge[turn]]


def run_slots(mode, scalars, constants, window, total=None, sources=()):
    _, _, _, measured = constants
    slot_count, extent = measured.shape[:2]
    n = extent // 2
    tile = window.shape[1] - 2 * n
    square = (4, n, n)
    outs = {
        INSIDE: [(window.shape, FULL), ((2, extent, extent), FULL)],
        BESIDE: [((4, n, tile - 2 * n), HALF)],
        OVER: [((4, n, tile - 2 * n), HALF)],
        CORNER: [((2, *square), HALF)] * 2 + [((2, 2, *square), FULL)],
    }[mode]
    operands = [*scalars, *constants]
    specs = [SMEM, SMEM, VMEM, VMEM, VMEM, VMEM]
    aliases = {}
    if mode == INSIDE:
        operands += [window]
        specs += [VMEM]
    else:
        operands += [*sources, window, total]
        specs += [VMEM] * (len(sources) + 2)
        aliases = {6 + len(sources): 0, 7 + len(sources): 1}
        outs = [(window.shape, HALF), (total.shape, FULL)] + outs
    return pl.pallas_call(
        functools.partial(slots_kernel, mode),
        out_shape=[jax.ShapeDtypeStruct(*out) for out in outs],
        in_specs=specs,
        out_specs=[VMEM] * len(outs),
        scratch_shapes=[pltpu.SMEM((slot_count + 3,), jnp.int32)],
        input_output_aliases=aliases,
        compiler_params=pltpu.CompilerParams(vmem_limit_bytes=24 << 20),
        cost_estimate=pl.CostEstimate(
            flops=3 * 52 * extent**3, bytes_accessed=0, transcendentals=0
        ),
    )(*operands)


def turn_kernel(n, first, second, token, *outs):
    planes, _, tile = first.shape
    for turn in range(2):
        cols = pick(ahead("col", turn), 0, tile - n, n)
        for d, band in enumerate((first, second)):
            for k in range(planes):
                outs[turn][d, k] = band[k, :, cols]


def turn_ends(first, second, token):
    planes, n, _ = first.shape
    out = jax.ShapeDtypeStruct((2, planes, n, n), HALF)
    return pl.pallas_call(
        functools.partial(turn_kernel, n),
        out_shape=[out, out],
        in_specs=[VMEM] * 3,
        out_specs=[VMEM] * 2,
        compiler_params=pltpu.CompilerParams(vmem_limit_bytes=8 << 20),
        name="turn",
    )(first, second, token)


def sides_kernel(n, total, *outs):
    planes, tile = outs[0].shape[:2]
    for turn in range(2):
        cols = pick(ahead("col", turn), 0, n + tile, n)
        for k in range(planes):
            outs[turn][k] = total[k, pl.ds(n, tile), cols].astype(HALF)


def sides(total, n):
    out = jax.ShapeDtypeStruct((total.shape[0], total.shape[1] - 2 * n, n), HALF)
    return pl.pallas_call(
        functools.partial(sides_kernel, n),
        out_shape=[out, out],
        in_specs=[VMEM],
        out_specs=[VMEM] * 2,
        compiler_params=pltpu.CompilerParams(vmem_limit_bytes=8 << 20),
        name="sides",
    )(total)


def join_kernel(edge, first, second, *outs):
    for d, out in enumerate(outs):
        out[0] = (edge[d, 0] + first[d].astype(FULL)).astype(HALF)
        out[1] = (edge[d, 1] + second[d].astype(FULL)).astype(HALF)


def join(edge, first, second):
    out = jax.ShapeDtypeStruct(edge.shape[1:], HALF)
    return pl.pallas_call(
        join_kernel,
        out_shape=[out, out],
        in_specs=[VMEM] * 3,
        out_specs=[VMEM] * 2,
        compiler_params=pltpu.CompilerParams(vmem_limit_bytes=8 << 20),
        name="join",
    )(edge, first, second)


def settle_kernel(n, first, second, total_in, total, out, sems):
    tile = out.shape[1]
    for turn, side in enumerate((first, second)):
        cols = pick(ahead("col", turn), n, tile, n)
        for k in range(out.shape[0]):
            total[k, pl.ds(n, tile), cols] += side[k].astype(FULL)
    rows = tile - 2 * n
    run_copies([(total.at[:, pl.ds(2 * n, rows), pl.ds(n, tile)], out.at[:, pl.ds(n, rows)])], sems)


def settle(total, first, second, n):
    planes, tile = first.shape[:2]
    return pl.pallas_call(
        functools.partial(settle_kernel, n),
        out_shape=[
            jax.ShapeDtypeStruct(total.shape, FULL),
            jax.ShapeDtypeStruct((planes, tile, tile), FULL),
        ],
        in_specs=[VMEM] * 3,
        out_specs=[VMEM, ANYWHERE],
        scratch_shapes=[pltpu.SemaphoreType.DMA((1,))],
        input_output_aliases={2: 0},
        compiler_params=pltpu.CompilerParams(vmem_limit_bytes=16 << 20),
        name="settle",
    )(first, second, total)


def finish_kernel(n, core_0, core_1, edge_0, edge_1, total, out_in, out, band, sems):
    planes, tile = out.shape[:2]
    copies = []
    for turn, (core, edge) in enumerate(((core_0, edge_0), (core_1, edge_1))):
        side = ahead("row", turn)
        rows = pick(side, n, tile, n)
        to = pick(side, 0, tile - n, n)
        for k in range(planes):
            band[turn, k, :, pl.ds(n, tile - 2 * n)] = total[
                k, rows, pl.ds(2 * n, tile - 2 * n)
            ] + core[k].astype(FULL)
            for e in range(2):
                at = ahead("col", e)
                band[turn, k, :, pick(at, 0, tile - n, n)] = total[
                    k, rows, pick(at, n, tile, n)
                ] + edge[e, k].astype(FULL)
            copies.append(
                pltpu.make_async_copy(
                    band.at[turn, k], out.at[k, to], sems.at[turn * planes + k]
                )
            )
            copies[-1].start()
    for copy in copies:
        copy.wait()


def finish(total, out, cores, edges, n):
    planes, tile = out.shape[:2]
    return pl.pallas_call(
        functools.partial(finish_kernel, n),
        out_shape=jax.ShapeDtypeStruct(out.shape, FULL),
        in_specs=[VMEM] * 5 + [ANYWHERE],
        out_specs=ANYWHERE,
        scratch_shapes=[
            pltpu.VMEM((2, planes, n, tile), FULL),
            pltpu.SemaphoreType.DMA((2 * planes,)),
        ],
        input_output_aliases={5: 0},
        compiler_params=pltpu.CompilerParams(vmem_limit_bytes=16 << 20),
        name="finish",
    )(*cores, *edges, total, out)


def both(parts, axis):
    return [exchange(part, axis, turn) for turn, part in enumerate(parts)]


def per_device(objects, illumination, propagator_phase, intensity, offsets, counts):
    extent = intensity.shape[1]
    n = extent // 2
    scalars = (offsets.T, counts)
    window, *strips = prepare(objects, n)
    over = both(strips[:2], "row")
    beside = both(strips[2:], "col")
    constants = [jnp.asarray(half_tables(extent)), illumination, propagator_phase, intensity]
    total, constants[2] = run_slots(INSIDE, scalars, constants, window)
    window, total, core = run_slots(BESIDE, scalars, constants, window, total, (*beside, over[0]))
    cores = [exchange(core, "row", 0)]
    corner = both(turn_ends(*over, core), "col")
    window, total, core = run_slots(OVER, scalars, constants, window, total, over[1:])
    cores += [exchange(core, "row", 1)]
    _, total, *ends, edge = run_slots(CORNER, scalars, constants, window, total, corner)
    ends = both(ends, "col")
    outer = both(sides(total, n), "col")
    edges = both(join(edge, *ends), "row")
    total, out = settle(total, *outer, n)
    return finish(total, out, cores, edges, n)


def solution(mesh):
    placed = (
        P(None, "row", "col"),
        P(),
        P(),
        P(("row", "col"), None, None),
        P(("row", "col"), None),
        P(("row", "col")),
    )
    return jax.shard_map(
        per_device, mesh=mesh, in_specs=placed, out_specs=P(None, "row", "col"), check_vma=False
    )
```

```python
import functools
import math

import jax
import jax.numpy as jnp
import numpy as np
from jax import lax
from jax.experimental import pallas as pl
from jax.experimental.pallas import tpu as pltpu
from jax.sharding import PartitionSpec as P


HALF = jnp.bfloat16
FULL = jnp.float32


def exchange(x, axis, turn):
    size = lax.axis_size(axis)
    pairs = [(i, i + 1) for i in range(turn, size - 1, 2)]
    return lax.ppermute(x, axis, pairs + [(j, i) for i, j in pairs])


def ahead(axis, turn):
    odd = lax.axis_index(axis) % 2
    return odd if turn == 0 else 1 - odd


def pick(side, low, high, size):
    return pl.ds(pl.multiple_of(high - side * (high - low), size), size)


def half_tables(extent):
    half = extent // 2
    number = np.arange(extent, dtype=np.int64)
    turns = (number[:, None] * number[None, :]) % extent
    angle = turns.astype(np.float32) * np.float32(2.0 * math.pi / extent)
    scale = np.float32(1.0 / math.sqrt(extent))
    cosine, sine = np.cos(angle) * scale, np.sin(angle) * scale
    tables = []
    for parity in range(2):
        c, s = cosine[parity::2, :half], sine[parity::2, :half]
        block = np.block([[c, s], [-s, c]])
        tables += [block, block.T]
    pick = np.zeros((extent, extent), np.float32)
    pick[number, np.concatenate([number[0::2], number[1::2]])] = 1.0
    tables += [pick, pick.T]
    return np.stack(tables).astype(HALF)


EVEN, EVEN_T, ODD, ODD_T, PICK, PICK_T = range(6)


def dot(left, right):
    return jnp.dot(left, right, preferred_element_type=FULL)


def beside(*parts):
    return jnp.concatenate(parts, axis=1)


def above(*parts):
    return jnp.concatenate(parts, axis=0)


def stacked(fields, table):
    rows = fields[0].shape[0]
    result = dot(above(*fields) if len(fields) > 1 else fields[0], table)
    return [result[i * rows : (i + 1) * rows] for i in range(len(fields))]


def crossed(fields):
    return [x.astype(HALF).T for x in fields]


def paired(firsts, seconds, side, n):
    cols = slice(side * n, side * n + n)
    return [
        above(beside(x[:n, cols], x[n:, cols]), beside(y[:n, cols], y[n:, cols]))
        for x, y in zip(firsts, seconds)
    ]


def butterfly(x, n):
    y = above(x[:n] + x[n:], x[:n] - x[n:])
    return beside(y[:, :n] + y[:, n:], y[:, :n] - y[:, n:]).astype(HALF)


def forward(fields, tab, n):
    fields = [(butterfly(real, n), butterfly(imag, n)) for real, imag in fields]
    even = stacked([beside(r[:, :n], i[:, :n]) for r, i in fields], tab[EVEN_T])
    odd = stacked([beside(r[:, n:], i[:, n:]) for r, i in fields], tab[ODD_T])
    even, odd = crossed(even), crossed(odd)
    return (
        stacked(paired(even, odd, 0, n), tab[EVEN_T]),
        stacked(paired(even, odd, 1, n), tab[ODD_T]),
    )


def inverse(even, odd, tab, n):
    first = crossed(stacked(even, tab[EVEN]))
    second = crossed(stacked(odd, tab[ODD]))
    even = stacked(paired(first, second, 0, n), tab[EVEN])
    odd = stacked(paired(first, second, 1, n), tab[ODD])
    fields = []
    for x, y in zip(even, odd):
        low, high = [above(z[:n] + z[n:], z[:n] - z[n:]) for z in (x + y, x - y)]
        fields.append((beside(low[:, :n], high[:, :n]), beside(low[:, n:], high[:, n:])))
    return fields


def times(a, b):
    return a[0] * b[0] - a[1] * b[1], a[0] * b[1] + a[1] * b[0]


def times_conjugate(a, b):
    return a[0] * b[0] + a[1] * b[1], a[0] * b[1] - a[1] * b[0]


def slot_group(light, spread, planes, measured, tab, puts, n):
    def turned(fields, col, product):
        h = spread(col)
        pairs = [product(h, (y[:, :n], y[:, n:])) for y in fields]
        return [beside(real.astype(HALF), imag.astype(HALF)) for real, imag in pairs]

    def pull(fields, levels, col):
        results = []
        for y, level in zip(fields, levels):
            real, imag = y[:, :n], y[:, n:]
            misfit = real * real + imag * imag - level[:, col : col + n]
            results.append(beside((misfit * real).astype(HALF), (misfit * imag).astype(HALF)))
        return results

    even, odd = forward([times(light(), plane(0)) for plane in planes], tab, n)
    passed = inverse(turned(even, 0, times), turned(odd, n, times), tab, n)
    even, odd = forward([times(x, plane(2)) for x, plane in zip(passed, planes)], tab, n)
    levels = crossed(stacked([level() for level in measured], tab[PICK_T]))
    levels = stacked(levels, tab[PICK_T])
    back = inverse(pull(even, levels, 0), pull(odd, levels, n), tab, n)
    for put, x, y in zip(puts, passed, back):
        put(2, times_conjugate(x, y))
    even, odd = forward([times_conjugate(plane(2), y) for plane, y in zip(planes, back)], tab, n)
    start = inverse(
        turned(even, 0, times_conjugate), turned(odd, n, times_conjugate), tab, n
    )
    for put, y in zip(puts, start):
        put(0, times_conjugate(light(), y))


def wave_of(phase):
    half = phase * 0.5
    square = half * half
    sine, cosine = 0.0, 0.0
    for k in range(6, -1, -1):
        cosine = cosine * square + (-1.0) ** k / math.factorial(2 * k)
        sine = sine * square + (-1.0) ** k / math.factorial(2 * k + 1)
    sine = sine * half
    return 1.0 - 2.0 * sine * sine, 2.0 * sine * cosine


def selected(x, tab):
    result = None
    for _ in range(3):
        part = x.astype(HALF)
        x = x - part.astype(FULL)
        moved = dot(dot(tab[PICK], part).astype(HALF), tab[PICK_T])
        result = moved if result is None else result + moved
    return result


INSIDE, BESIDE, OVER, CORNER = range(4)
VMEM = pl.BlockSpec(memory_space=pltpu.VMEM)
SMEM = pl.BlockSpec(memory_space=pltpu.SMEM)
ANYWHERE = pl.BlockSpec(memory_space=pl.ANY)


def run_copies(moves, sems):
    copies = [
        pltpu.make_async_copy(source, target, sems.at[i])
        for i, (source, target) in enumerate(moves)
    ]
    for copy in copies:
        copy.start()
    for copy in copies:
        copy.wait()


def prepare_kernel(n, objects, window, *strips):
    planes, tile = objects.shape[:2]
    for k in range(planes):
        window[k, n : n + tile, n : n + tile] = objects[k].astype(HALF)
    for turn in range(2):
        rows = pick(ahead("row", turn), 0, tile - n, n)
        cols = pick(ahead("col", turn), 0, tile - n, n)
        for k in range(planes):
            strips[turn][k] = objects[k, rows, :].astype(HALF)
            strips[2 + turn][k] = objects[k, :, cols].astype(HALF)


def prepare(objects, n):
    planes, tile = objects.shape[:2]
    flat = jax.ShapeDtypeStruct((planes, n, tile), HALF)
    tall = jax.ShapeDtypeStruct((planes, tile, n), HALF)
    whole = jax.ShapeDtypeStruct((planes, tile + 2 * n, tile + 2 * n), HALF)
    return pl.pallas_call(
        functools.partial(prepare_kernel, n),
        in_specs=[VMEM],
        out_specs=[VMEM] * 5,
        out_shape=[whole, flat, flat, tall, tall],
        compiler_params=pltpu.CompilerParams(vmem_limit_bytes=16 << 20),
        cost_estimate=pl.CostEstimate(
            flops=2000 * objects.size, bytes_accessed=6 * objects.size, transcendentals=0
        ),
        name="prepare",
    )(objects)


def slots_kernel(mode, offsets, counts, tab, light, spread, measured, *refs):
    order = refs[-1]
    slot_count, extent = measured.shape[:2]
    n = extent // 2
    if mode == INSIDE:
        window, total, spread_out = refs[:3]
    else:
        m = {BESIDE: 3, OVER: 1, CORNER: 2}[mode]
        sources, (window, total), outs = refs[:m], refs[m + 2 : m + 4], refs[m + 4 : -1]
    tile = window.shape[1] - 2 * n
    inner = pl.ds(n, tile)
    row_halo = [pick(ahead("row", turn), 0, n + tile, n) for turn in range(2)]
    col_halo = [pick(ahead("col", turn), 0, n + tile, n) for turn in range(2)]
    col_edge = [pick(ahead("col", turn), n, tile, n) for turn in range(2)]

    if mode == INSIDE:

        def clear(i, carry):
            at = pl.ds(pl.multiple_of(32 * i, 32), 32)
            total[:, at] = jnp.zeros((4, 32, total.shape[2]), FULL)
            return carry

        lax.fori_loop(0, total.shape[1] // 32, clear, 0)
        for k, wave in enumerate(wave_of(spread[...].T)):
            spread_out[k] = selected(wave, tab)
        spread = spread_out
    else:
        if mode == BESIDE:
            moves = [(sources[turn], (inner, col_halo[turn])) for turn in range(2)]
            moves += [(sources[2], (row_halo[0], inner))]
        elif mode == OVER:
            moves = [(sources[0], (row_halo[1], inner))]
        else:
            moves = [
                (sources[turn].at[d], (row_halo[d], col_halo[turn]))
                for turn in range(2)
                for d in range(2)
            ]
        for source, at in moves:
            for k in range(4):
                window[(k, *at)] = source[k]

    def inside(at):
        return (at >= 0) & ((at + 2) * n <= tile)

    def listed(kind, found):
        for j in range(slot_count):
            row, col = offsets[0, j], offsets[1, j]
            early = inside(row) | ((row < 0) == (ahead("row", 0) == 1))
            wanted = j < counts[0]
            if kind == INSIDE:
                wanted &= inside(row) & inside(col)
            elif kind == BESIDE:
                wanted &= (inside(row) != inside(col)) & early
            elif kind == OVER:
                wanted &= jnp.logical_not(early) & inside(col)
            else:
                wanted &= jnp.logical_not(inside(row) | inside(col))
            order[found] = j
            found = found + wanted.astype(jnp.int32)
        return found

    group = 3 if mode in (INSIDE, BESIDE) else 2
    found = jnp.int32(0)
    if mode == BESIDE:
        found = listed(INSIDE, found)
        left = found % group
        for i in range(group - 1):
            order[i] = order[jnp.maximum(found - left + i, 0)]
        found = left
    found = listed(mode, found)

    def run(at, size):
        planes, puts, measures = [], [], []
        for i in range(size):
            slot = order[jnp.minimum(at + i, found - 1)]
            row = pl.multiple_of((offsets[0, slot] + 1) * n, n)
            col = pl.multiple_of((offsets[1, slot] + 1) * n, n)

            def plane(k, here=(pl.ds(row, extent), pl.ds(col, extent))):
                return window[(k, *here)].astype(FULL), window[(k + 1, *here)].astype(FULL)

            def put(k, pair, here=(pl.ds(row, extent), pl.ds(col, extent)), i=i):
                for part in range(2):
                    value = pair[part]
                    if mode == BESIDE and i == size - 1 and size > 1:
                        value = jnp.where(at + i < found, value, 0.0)
                    total[(k + part, *here)] += value

            planes.append(plane)
            puts.append(put)
            measures.append(lambda slot=slot: measured[slot])
        slot_group(
            lambda: (light[0], light[1]),
            lambda col: (spread[0, :, col : col + n], spread[1, :, col : col + n]),
            planes,
            measures,
            tab,
            puts,
            n,
        )

    def several(i, carry):
        run(group * i, group)
        return carry

    spare = 1 if mode == BESIDE else 0
    lax.fori_loop(0, (found + spare) // group, several, 0)
    if mode != INSIDE:

        @pl.when(found % group == 1)
        def _():
            run(found - 1, 1)

    if mode in (BESIDE, OVER):
        rows = row_halo[0 if mode == BESIDE else 1]
        for k in range(4):
            outs[0][k] = total[k, rows, pl.ds(2 * n, tile - 2 * n)].astype(HALF)
    if mode == CORNER:
        ends, edge = outs[:2], outs[2]
        for turn in range(2):
            for d in range(2):
                for k in range(4):
                    ends[turn][d, k] = total[k, row_halo[d], col_halo[turn]].astype(HALF)
                    edge[d, turn, k] = total[k, row_halo[d], col_edge[turn]]


def run_slots(mode, scalars, constants, window, total=None, sources=()):
    _, _, _, measured = constants
    slot_count, extent = measured.shape[:2]
    n = extent // 2
    tile = window.shape[1] - 2 * n
    square = (4, n, n)
    outs = {
        INSIDE: [(window.shape, FULL), ((2, extent, extent), FULL)],
        BESIDE: [((4, n, tile - 2 * n), HALF)],
        OVER: [((4, n, tile - 2 * n), HALF)],
        CORNER: [((2, *square), HALF)] * 2 + [((2, 2, *square), FULL)],
    }[mode]
    operands = [*scalars, *constants]
    specs = [SMEM, SMEM, VMEM, VMEM, VMEM, VMEM]
    aliases = {}
    if mode == INSIDE:
        operands += [window]
        specs += [VMEM]
    else:
        operands += [*sources, window, total]
        specs += [VMEM] * (len(sources) + 2)
        aliases = {6 + len(sources): 0, 7 + len(sources): 1}
        outs = [(window.shape, HALF), (total.shape, FULL)] + outs
    return pl.pallas_call(
        functools.partial(slots_kernel, mode),
        out_shape=[jax.ShapeDtypeStruct(*out) for out in outs],
        in_specs=specs,
        out_specs=[VMEM] * len(outs),
        scratch_shapes=[pltpu.SMEM((slot_count + 3,), jnp.int32)],
        input_output_aliases=aliases,
        compiler_params=pltpu.CompilerParams(vmem_limit_bytes=24 << 20),
        cost_estimate=pl.CostEstimate(
            flops=3 * 52 * extent**3, bytes_accessed=0, transcendentals=0
        ),
    )(*operands)


def turn_kernel(n, first, second, token, *outs):
    planes, _, tile = first.shape
    for turn in range(2):
        cols = pick(ahead("col", turn), 0, tile - n, n)
        for d, band in enumerate((first, second)):
            for k in range(planes):
                outs[turn][d, k] = band[k, :, cols]


def turn_ends(first, second, token):
    planes, n, _ = first.shape
    out = jax.ShapeDtypeStruct((2, planes, n, n), HALF)
    return pl.pallas_call(
        functools.partial(turn_kernel, n),
        out_shape=[out, out],
        in_specs=[VMEM] * 3,
        out_specs=[VMEM] * 2,
        compiler_params=pltpu.CompilerParams(vmem_limit_bytes=8 << 20),
        name="turn",
    )(first, second, token)


def sides_kernel(n, total, *outs):
    planes, tile = outs[0].shape[:2]
    for turn in range(2):
        cols = pick(ahead("col", turn), 0, n + tile, n)
        for k in range(planes):
            outs[turn][k] = total[k, pl.ds(n, tile), cols].astype(HALF)


def sides(total, n):
    out = jax.ShapeDtypeStruct((total.shape[0], total.shape[1] - 2 * n, n), HALF)
    return pl.pallas_call(
        functools.partial(sides_kernel, n),
        out_shape=[out, out],
        in_specs=[VMEM],
        out_specs=[VMEM] * 2,
        compiler_params=pltpu.CompilerParams(vmem_limit_bytes=8 << 20),
        name="sides",
    )(total)


def join_kernel(edge, first, second, *outs):
    for d, out in enumerate(outs):
        out[0] = (edge[d, 0] + first[d].astype(FULL)).astype(HALF)
        out[1] = (edge[d, 1] + second[d].astype(FULL)).astype(HALF)


def join(edge, first, second):
    out = jax.ShapeDtypeStruct(edge.shape[1:], HALF)
    return pl.pallas_call(
        join_kernel,
        out_shape=[out, out],
        in_specs=[VMEM] * 3,
        out_specs=[VMEM] * 2,
        compiler_params=pltpu.CompilerParams(vmem_limit_bytes=8 << 20),
        name="join",
    )(edge, first, second)


def settle_kernel(n, side_0, side_1, core_0, core_1, total_in, total, out, sems):
    planes, tile = out.shape[:2]
    inner, middle = pl.ds(n, tile), pl.ds(2 * n, tile - 2 * n)
    for turn, (side, core) in enumerate(((side_0, core_0), (side_1, core_1))):
        cols = pick(ahead("col", turn), n, tile, n)
        rows = pick(ahead("row", turn), n, tile, n)
        for k in range(planes):
            total[k, inner, cols] += side[k].astype(FULL)
            total[k, rows, middle] += core[k].astype(FULL)
    moves = [(total.at[:, middle, inner], out.at[:, pl.ds(n, tile - 2 * n)])]
    for at in (0, tile - n):
        band = total.at[:, pl.ds(n + at, n), middle]
        moves.append((band, out.at[:, pl.ds(at, n), pl.ds(n, tile - 2 * n)]))
    run_copies(moves, sems)


def settle(total, sides, cores, n):
    planes, tile = sides[0].shape[:2]
    return pl.pallas_call(
        functools.partial(settle_kernel, n),
        out_shape=[
            jax.ShapeDtypeStruct(total.shape, FULL),
            jax.ShapeDtypeStruct((planes, tile, tile), FULL),
        ],
        in_specs=[VMEM] * 5,
        out_specs=[VMEM, ANYWHERE],
        scratch_shapes=[pltpu.SemaphoreType.DMA((3,))],
        input_output_aliases={4: 0},
        compiler_params=pltpu.CompilerParams(vmem_limit_bytes=16 << 20),
        name="settle",
    )(*sides, *cores, total)


def finish_kernel(n, edge_0, edge_1, total, out_in, out, block, sems):
    planes, tile = out.shape[:2]
    copies = []
    for turn, edge in enumerate((edge_0, edge_1)):
        for e in range(2):
            row, col = ahead("row", turn), ahead("col", e)
            rows, cols = pick(row, n, tile, n), pick(col, n, tile, n)
            for k in range(planes):
                block[turn, e, k] = total[k, rows, cols] + edge[e, k].astype(FULL)
            target = out.at[:, pick(row, 0, tile - n, n), pick(col, 0, tile - n, n)]
            copies.append(pltpu.make_async_copy(block.at[turn, e], target, sems.at[2 * turn + e]))
            copies[-1].start()
    for copy in copies:
        copy.wait()


def finish(total, out, edges, n):
    planes = out.shape[0]
    return pl.pallas_call(
        functools.partial(finish_kernel, n),
        out_shape=jax.ShapeDtypeStruct(out.shape, FULL),
        in_specs=[VMEM] * 3 + [ANYWHERE],
        out_specs=ANYWHERE,
        scratch_shapes=[pltpu.VMEM((2, 2, planes, n, n), FULL), pltpu.SemaphoreType.DMA((4,))],
        input_output_aliases={3: 0},
        compiler_params=pltpu.CompilerParams(vmem_limit_bytes=16 << 20),
        name="finish",
    )(*edges, total, out)


def both(parts, axis):
    return [exchange(part, axis, turn) for turn, part in enumerate(parts)]


def per_device(objects, illumination, propagator_phase, intensity, offsets, counts):
    extent = intensity.shape[1]
    n = extent // 2
    scalars = (offsets.T, counts)
    window, *strips = prepare(objects, n)
    over = both(strips[:2], "row")
    beside = both(strips[2:], "col")
    constants = [jnp.asarray(half_tables(extent)), illumination, propagator_phase, intensity]
    total, constants[2] = run_slots(INSIDE, scalars, constants, window)
    window, total, core = run_slots(BESIDE, scalars, constants, window, total, (*beside, over[0]))
    cores = [exchange(core, "row", 0)]
    corner = both(turn_ends(*over, core), "col")
    window, total, core = run_slots(OVER, scalars, constants, window, total, over[1:])
    cores += [exchange(core, "row", 1)]
    _, total, *ends, edge = run_slots(CORNER, scalars, constants, window, total, corner)
    ends = both(ends, "col")
    outer = both(sides(total, n), "col")
    edges = both(join(edge, *ends), "row")
    total, out = settle(total, outer, cores, n)
    return finish(total, out, edges, n)


def solution(mesh):
    placed = (
        P(None, "row", "col"),
        P(),
        P(),
        P(("row", "col"), None, None),
        P(("row", "col"), None),
        P(("row", "col")),
    )
    return jax.shard_map(
        per_device, mesh=mesh, in_specs=placed, out_specs=P(None, "row", "col"), check_vma=False
    )
```

```python
import functools
import math

import jax
import jax.numpy as jnp
import numpy as np
from jax import lax
from jax.experimental import pallas as pl
from jax.experimental.pallas import tpu as pltpu
from jax.sharding import PartitionSpec as P


HALF = jnp.bfloat16
FULL = jnp.float32


def exchange(x, axis, turn):
    size = lax.axis_size(axis)
    pairs = [(i, i + 1) for i in range(turn, size - 1, 2)]
    return lax.ppermute(x, axis, pairs + [(j, i) for i, j in pairs])


def ahead(axis, turn):
    odd = lax.axis_index(axis) % 2
    return odd if turn == 0 else 1 - odd


def pick(side, low, high, size):
    return pl.ds(pl.multiple_of(high - side * (high - low), size), size)


def half_tables(extent):
    half = extent // 2
    number = np.arange(extent, dtype=np.int64)
    turns = (number[:, None] * number[None, :]) % extent
    angle = turns.astype(np.float32) * np.float32(2.0 * math.pi / extent)
    scale = np.float32(1.0 / math.sqrt(extent))
    cosine, sine = np.cos(angle) * scale, np.sin(angle) * scale
    tables = []
    for parity in range(2):
        c, s = cosine[parity::2, :half], sine[parity::2, :half]
        block = np.block([[c, s], [-s, c]])
        tables += [block, block.T]
    pick = np.zeros((extent, extent), np.float32)
    pick[number, np.concatenate([number[0::2], number[1::2]])] = 1.0
    tables += [pick, pick.T]
    return np.stack(tables).astype(HALF)


EVEN, EVEN_T, ODD, ODD_T, PICK, PICK_T = range(6)


def dot(left, right):
    return jnp.dot(left, right, preferred_element_type=FULL)


def beside(*parts):
    return jnp.concatenate(parts, axis=1)


def above(*parts):
    return jnp.concatenate(parts, axis=0)


def stacked(fields, table):
    rows = fields[0].shape[0]
    result = dot(above(*fields) if len(fields) > 1 else fields[0], table)
    return [result[i * rows : (i + 1) * rows] for i in range(len(fields))]


def crossed(fields):
    return [x.astype(HALF).T for x in fields]


def paired(firsts, seconds, side, n):
    cols = slice(side * n, side * n + n)
    return [
        above(beside(x[:n, cols], x[n:, cols]), beside(y[:n, cols], y[n:, cols]))
        for x, y in zip(firsts, seconds)
    ]


def butterfly(x, n):
    y = above(x[:n] + x[n:], x[:n] - x[n:])
    return beside(y[:, :n] + y[:, n:], y[:, :n] - y[:, n:]).astype(HALF)


def forward(fields, tab, n):
    fields = [(butterfly(real, n), butterfly(imag, n)) for real, imag in fields]
    even = stacked([beside(r[:, :n], i[:, :n]) for r, i in fields], tab[EVEN_T])
    odd = stacked([beside(r[:, n:], i[:, n:]) for r, i in fields], tab[ODD_T])
    even, odd = crossed(even), crossed(odd)
    return (
        stacked(paired(even, odd, 0, n), tab[EVEN_T]),
        stacked(paired(even, odd, 1, n), tab[ODD_T]),
    )


def inverse(even, odd, tab, n):
    first = crossed(stacked(even, tab[EVEN]))
    second = crossed(stacked(odd, tab[ODD]))
    even = stacked(paired(first, second, 0, n), tab[EVEN])
    odd = stacked(paired(first, second, 1, n), tab[ODD])
    fields = []
    for x, y in zip(even, odd):
        low, high = [above(z[:n] + z[n:], z[:n] - z[n:]) for z in (x + y, x - y)]
        fields.append((beside(low[:, :n], high[:, :n]), beside(low[:, n:], high[:, n:])))
    return fields


def times(a, b):
    return a[0] * b[0] - a[1] * b[1], a[0] * b[1] + a[1] * b[0]


def times_conjugate(a, b):
    return a[0] * b[0] + a[1] * b[1], a[0] * b[1] - a[1] * b[0]


def slot_group(light, spread, planes, measured, tab, puts, n):
    def turned(fields, col, product):
        h = spread(col)
        pairs = [product(h, (y[:, :n], y[:, n:])) for y in fields]
        return [beside(real.astype(HALF), imag.astype(HALF)) for real, imag in pairs]

    def pull(fields, levels, col):
        results = []
        for y, level in zip(fields, levels):
            real, imag = y[:, :n], y[:, n:]
            misfit = real * real + imag * imag - level[:, col : col + n]
            results.append(beside((misfit * real).astype(HALF), (misfit * imag).astype(HALF)))
        return results

    even, odd = forward([times(light(), plane(0)) for plane in planes], tab, n)
    passed = inverse(turned(even, 0, times), turned(odd, n, times), tab, n)
    even, odd = forward([times(x, plane(2)) for x, plane in zip(passed, planes)], tab, n)
    levels = crossed(stacked([level() for level in measured], tab[PICK_T]))
    levels = stacked(levels, tab[PICK_T])
    back = inverse(pull(even, levels, 0), pull(odd, levels, n), tab, n)
    for put, x, y in zip(puts, passed, back):
        put(2, times_conjugate(x, y))
    even, odd = forward([times_conjugate(plane(2), y) for plane, y in zip(planes, back)], tab, n)
    start = inverse(
        turned(even, 0, times_conjugate), turned(odd, n, times_conjugate), tab, n
    )
    for put, y in zip(puts, start):
        put(0, times_conjugate(light(), y))


def wave_of(phase):
    half = phase * 0.5
    square = half * half
    sine, cosine = 0.0, 0.0
    for k in range(6, -1, -1):
        cosine = cosine * square + (-1.0) ** k / math.factorial(2 * k)
        sine = sine * square + (-1.0) ** k / math.factorial(2 * k + 1)
    sine = sine * half
    return 1.0 - 2.0 * sine * sine, 2.0 * sine * cosine


def selected(x, tab):
    result = None
    for _ in range(3):
        part = x.astype(HALF)
        x = x - part.astype(FULL)
        moved = dot(dot(tab[PICK], part).astype(HALF), tab[PICK_T])
        result = moved if result is None else result + moved
    return result


INSIDE, BESIDE, OVER, CORNER = range(4)
VMEM = pl.BlockSpec(memory_space=pltpu.VMEM)
SMEM = pl.BlockSpec(memory_space=pltpu.SMEM)
ANYWHERE = pl.BlockSpec(memory_space=pl.ANY)


def run_copies(moves, sems):
    copies = [
        pltpu.make_async_copy(source, target, sems.at[i])
        for i, (source, target) in enumerate(moves)
    ]
    for copy in copies:
        copy.start()
    for copy in copies:
        copy.wait()


def prepare_kernel(n, objects, window, *strips):
    planes, tile = objects.shape[:2]
    for k in range(planes):
        window[k, n : n + tile, n : n + tile] = objects[k].astype(HALF)
    for turn in range(2):
        rows = pick(ahead("row", turn), 0, tile - n, n)
        cols = pick(ahead("col", turn), 0, tile - n, n)
        for k in range(planes):
            strips[turn][k] = objects[k, rows, :].astype(HALF)
            strips[2 + turn][k] = objects[k, :, cols].astype(HALF)


def prepare(objects, n):
    planes, tile = objects.shape[:2]
    flat = jax.ShapeDtypeStruct((planes, n, tile), HALF)
    tall = jax.ShapeDtypeStruct((planes, tile, n), HALF)
    whole = jax.ShapeDtypeStruct((planes, tile + 2 * n, tile + 2 * n), HALF)
    return pl.pallas_call(
        functools.partial(prepare_kernel, n),
        in_specs=[VMEM],
        out_specs=[VMEM] * 5,
        out_shape=[whole, flat, flat, tall, tall],
        compiler_params=pltpu.CompilerParams(vmem_limit_bytes=16 << 20),
        cost_estimate=pl.CostEstimate(
            flops=2000 * objects.size, bytes_accessed=6 * objects.size, transcendentals=0
        ),
        name="prepare",
    )(objects)


def slots_kernel(mode, offsets, counts, tab, light, spread, measured, *refs):
    order = refs[-1]
    slot_count, extent = measured.shape[:2]
    n = extent // 2
    if mode == INSIDE:
        window, total, spread_out = refs[:3]
    else:
        m = {BESIDE: 3, OVER: 1, CORNER: 2}[mode]
        sources, (window, total), outs = refs[:m], refs[m + 2 : m + 4], refs[m + 4 : -1]
    tile = window.shape[1] - 2 * n
    inner = pl.ds(n, tile)
    row_halo = [pick(ahead("row", turn), 0, n + tile, n) for turn in range(2)]
    col_halo = [pick(ahead("col", turn), 0, n + tile, n) for turn in range(2)]
    col_edge = [pick(ahead("col", turn), n, tile, n) for turn in range(2)]

    if mode == INSIDE:

        def clear(i, carry):
            at = pl.ds(pl.multiple_of(32 * i, 32), 32)
            total[:, at] = jnp.zeros((4, 32, total.shape[2]), FULL)
            return carry

        lax.fori_loop(0, total.shape[1] // 32, clear, 0)
        for k, wave in enumerate(wave_of(spread[...].T)):
            spread_out[k] = selected(wave, tab)
        spread = spread_out
    else:
        if mode == BESIDE:
            moves = [(sources[turn], (inner, col_halo[turn])) for turn in range(2)]
            moves += [(sources[2], (row_halo[0], inner))]
        elif mode == OVER:
            moves = [(sources[0], (row_halo[1], inner))]
        else:
            moves = [
                (sources[turn].at[d], (row_halo[d], col_halo[turn]))
                for turn in range(2)
                for d in range(2)
            ]
        for source, at in moves:
            for k in range(4):
                window[(k, *at)] = source[k]

    def inside(at):
        return (at >= 0) & ((at + 2) * n <= tile)

    def listed(kind, found):
        for j in range(slot_count):
            row, col = offsets[0, j], offsets[1, j]
            early = inside(row) | ((row < 0) == (ahead("row", 0) == 1))
            wanted = j < counts[0]
            if kind == INSIDE:
                wanted &= inside(row) & inside(col)
            elif kind == BESIDE:
                wanted &= (inside(row) != inside(col)) & early
            elif kind == OVER:
                wanted &= jnp.logical_not(early) & inside(col)
            else:
                wanted &= jnp.logical_not(inside(row) | inside(col))
            order[found] = j
            found = found + wanted.astype(jnp.int32)
        return found

    group = 3 if mode in (INSIDE, BESIDE) else 2
    found = jnp.int32(0)
    if mode == BESIDE:
        found = listed(INSIDE, found)
        left = jnp.where(found < group, 0, found % group)
        for i in range(group - 1):
            order[i] = order[jnp.maximum(found - left + i, 0)]
        found = left
    found = listed(mode, found)

    def run(at, size):
        planes, puts, measures = [], [], []
        for i in range(size):
            slot = order[jnp.minimum(at + i, found - 1)]
            row = pl.multiple_of((offsets[0, slot] + 1) * n, n)
            col = pl.multiple_of((offsets[1, slot] + 1) * n, n)

            def plane(k, here=(pl.ds(row, extent), pl.ds(col, extent))):
                return window[(k, *here)].astype(FULL), window[(k + 1, *here)].astype(FULL)

            def put(k, pair, here=(pl.ds(row, extent), pl.ds(col, extent)), i=i):
                for part in range(2):
                    value = pair[part]
                    if i >= {INSIDE: 1, BESIDE: 2}.get(mode, size):
                        value = jnp.where(at + i < found, value, 0.0)
                    total[(k + part, *here)] += value

            planes.append(plane)
            puts.append(put)
            measures.append(lambda slot=slot: measured[slot])
        slot_group(
            lambda: (light[0], light[1]),
            lambda col: (spread[0, :, col : col + n], spread[1, :, col : col + n]),
            planes,
            measures,
            tab,
            puts,
            n,
        )

    def several(i, carry):
        run(group * i, group)
        return carry

    groups = (found + (1 if mode == BESIDE else 0)) // group
    if mode == INSIDE:
        groups = jnp.maximum(groups, jnp.minimum(found, 1))
    lax.fori_loop(0, groups, several, 0)
    if mode != INSIDE:

        @pl.when(found % group == 1)
        def _():
            run(found - 1, 1)

    if mode in (BESIDE, OVER):
        rows = row_halo[0 if mode == BESIDE else 1]
        for k in range(4):
            outs[0][k] = total[k, rows, pl.ds(2 * n, tile - 2 * n)].astype(HALF)
    if mode == CORNER:
        ends, edge = outs[:2], outs[2]
        for turn in range(2):
            for d in range(2):
                for k in range(4):
                    ends[turn][d, k] = total[k, row_halo[d], col_halo[turn]].astype(HALF)
                    edge[d, turn, k] = total[k, row_halo[d], col_edge[turn]]


def run_slots(mode, scalars, constants, window, total=None, sources=()):
    _, _, _, measured = constants
    slot_count, extent = measured.shape[:2]
    n = extent // 2
    tile = window.shape[1] - 2 * n
    square = (4, n, n)
    outs = {
        INSIDE: [(window.shape, FULL), ((2, extent, extent), FULL)],
        BESIDE: [((4, n, tile - 2 * n), HALF)],
        OVER: [((4, n, tile - 2 * n), HALF)],
        CORNER: [((2, *square), HALF)] * 2 + [((2, 2, *square), FULL)],
    }[mode]
    operands = [*scalars, *constants]
    specs = [SMEM, SMEM, VMEM, VMEM, VMEM, VMEM]
    aliases = {}
    if mode == INSIDE:
        operands += [window]
        specs += [VMEM]
    else:
        operands += [*sources, window, total]
        specs += [VMEM] * (len(sources) + 2)
        aliases = {6 + len(sources): 0, 7 + len(sources): 1}
        outs = [(window.shape, HALF), (total.shape, FULL)] + outs
    return pl.pallas_call(
        functools.partial(slots_kernel, mode),
        out_shape=[jax.ShapeDtypeStruct(*out) for out in outs],
        in_specs=specs,
        out_specs=[VMEM] * len(outs),
        scratch_shapes=[pltpu.SMEM((slot_count + 3,), jnp.int32)],
        input_output_aliases=aliases,
        compiler_params=pltpu.CompilerParams(vmem_limit_bytes=24 << 20),
        cost_estimate=pl.CostEstimate(
            flops=3 * 52 * extent**3, bytes_accessed=0, transcendentals=0
        ),
    )(*operands)


def turn_kernel(n, first, second, token, *outs):
    planes, _, tile = first.shape
    for turn in range(2):
        cols = pick(ahead("col", turn), 0, tile - n, n)
        for d, band in enumerate((first, second)):
            for k in range(planes):
                outs[turn][d, k] = band[k, :, cols]


def turn_ends(first, second, token):
    planes, n, _ = first.shape
    out = jax.ShapeDtypeStruct((2, planes, n, n), HALF)
    return pl.pallas_call(
        functools.partial(turn_kernel, n),
        out_shape=[out, out],
        in_specs=[VMEM] * 3,
        out_specs=[VMEM] * 2,
        compiler_params=pltpu.CompilerParams(vmem_limit_bytes=8 << 20),
        name="turn",
    )(first, second, token)


def sides_kernel(n, total, *outs):
    planes, tile = outs[0].shape[:2]
    for turn in range(2):
        cols = pick(ahead("col", turn), 0, n + tile, n)
        for k in range(planes):
            outs[turn][k] = total[k, pl.ds(n, tile), cols].astype(HALF)


def sides(total, n):
    out = jax.ShapeDtypeStruct((total.shape[0], total.shape[1] - 2 * n, n), HALF)
    return pl.pallas_call(
        functools.partial(sides_kernel, n),
        out_shape=[out, out],
        in_specs=[VMEM],
        out_specs=[VMEM] * 2,
        compiler_params=pltpu.CompilerParams(vmem_limit_bytes=8 << 20),
        name="sides",
    )(total)


def join_kernel(edge, first, second, *outs):
    for d, out in enumerate(outs):
        out[0] = (edge[d, 0] + first[d].astype(FULL)).astype(HALF)
        out[1] = (edge[d, 1] + second[d].astype(FULL)).astype(HALF)


def join(edge, first, second):
    out = jax.ShapeDtypeStruct(edge.shape[1:], HALF)
    return pl.pallas_call(
        join_kernel,
        out_shape=[out, out],
        in_specs=[VMEM] * 3,
        out_specs=[VMEM] * 2,
        compiler_params=pltpu.CompilerParams(vmem_limit_bytes=8 << 20),
        name="join",
    )(edge, first, second)


def settle_kernel(n, side_0, side_1, core_0, core_1, total_in, total, out, sems):
    planes, tile = out.shape[:2]
    inner, middle = pl.ds(n, tile), pl.ds(2 * n, tile - 2 * n)
    for turn, (side, core) in enumerate(((side_0, core_0), (side_1, core_1))):
        cols = pick(ahead("col", turn), n, tile, n)
        rows = pick(ahead("row", turn), n, tile, n)
        for k in range(planes):
            total[k, inner, cols] += side[k].astype(FULL)
            total[k, rows, middle] += core[k].astype(FULL)
    moves = [(total.at[:, middle, inner], out.at[:, pl.ds(n, tile - 2 * n)])]
    for at in (0, tile - n):
        band = total.at[:, pl.ds(n + at, n), middle]
        moves.append((band, out.at[:, pl.ds(at, n), pl.ds(n, tile - 2 * n)]))
    run_copies(moves, sems)


def settle(total, sides, cores, n):
    planes, tile = sides[0].shape[:2]
    return pl.pallas_call(
        functools.partial(settle_kernel, n),
        out_shape=[
            jax.ShapeDtypeStruct(total.shape, FULL),
            jax.ShapeDtypeStruct((planes, tile, tile), FULL),
        ],
        in_specs=[VMEM] * 5,
        out_specs=[VMEM, ANYWHERE],
        scratch_shapes=[pltpu.SemaphoreType.DMA((3,))],
        input_output_aliases={4: 0},
        compiler_params=pltpu.CompilerParams(vmem_limit_bytes=16 << 20),
        name="settle",
    )(*sides, *cores, total)


def finish_kernel(n, edge_0, edge_1, total, out_in, out, block, sems):
    planes, tile = out.shape[:2]
    copies = []
    for turn, edge in enumerate((edge_0, edge_1)):
        for e in range(2):
            row, col = ahead("row", turn), ahead("col", e)
            rows, cols = pick(row, n, tile, n), pick(col, n, tile, n)
            for k in range(planes):
                block[turn, e, k] = total[k, rows, cols] + edge[e, k].astype(FULL)
            target = out.at[:, pick(row, 0, tile - n, n), pick(col, 0, tile - n, n)]
            copies.append(pltpu.make_async_copy(block.at[turn, e], target, sems.at[2 * turn + e]))
            copies[-1].start()
    for copy in copies:
        copy.wait()


def finish(total, out, edges, n):
    planes = out.shape[0]
    return pl.pallas_call(
        functools.partial(finish_kernel, n),
        out_shape=jax.ShapeDtypeStruct(out.shape, FULL),
        in_specs=[VMEM] * 3 + [ANYWHERE],
        out_specs=ANYWHERE,
        scratch_shapes=[pltpu.VMEM((2, 2, planes, n, n), FULL), pltpu.SemaphoreType.DMA((4,))],
        input_output_aliases={3: 0},
        compiler_params=pltpu.CompilerParams(vmem_limit_bytes=16 << 20),
        name="finish",
    )(*edges, total, out)


def both(parts, axis):
    return [exchange(part, axis, turn) for turn, part in enumerate(parts)]


def per_device(objects, illumination, propagator_phase, intensity, offsets, counts):
    extent = intensity.shape[1]
    n = extent // 2
    scalars = (offsets.T, counts)
    window, *strips = prepare(objects, n)
    over = both(strips[:2], "row")
    beside = both(strips[2:], "col")
    constants = [jnp.asarray(half_tables(extent)), illumination, propagator_phase, intensity]
    total, constants[2] = run_slots(INSIDE, scalars, constants, window)
    window, total, core = run_slots(BESIDE, scalars, constants, window, total, (*beside, over[0]))
    cores = [exchange(core, "row", 0)]
    corner = both(turn_ends(*over, core), "col")
    window, total, core = run_slots(OVER, scalars, constants, window, total, over[1:])
    cores += [exchange(core, "row", 1)]
    _, total, *ends, edge = run_slots(CORNER, scalars, constants, window, total, corner)
    ends = both(ends, "col")
    outer = both(sides(total, n), "col")
    edges = both(join(edge, *ends), "row")
    total, out = settle(total, outer, cores, n)
    return finish(total, out, edges, n)


def solution(mesh):
    placed = (
        P(None, "row", "col"),
        P(),
        P(),
        P(("row", "col"), None, None),
        P(("row", "col"), None),
        P(("row", "col")),
    )
    return jax.shard_map(
        per_device, mesh=mesh, in_specs=placed, out_specs=P(None, "row", "col"), check_vma=False
    )
```
